128 devices in a mesh: row: 8 (over z, core), col: 16 (over y, x).
Axes of the slice: x: 4, y: 4, z: 4, core: 2. Of those that a mesh axis runs over, the one named last changes fastest.
Arguments:
- inputs: bfloat16 [512, 8192], P('row', 'col'), may hold values from -6 to 6
- grad_out: bfloat16 [512, 8192], P('row', 'col'), may hold values from -0.1796875 to 0.1796875
- gate_pre: bfloat16 [512, 28672], P('col', 'row'), may hold values from -6 to 6
- up_pre: bfloat16 [512, 28672], P('col', 'row'), may hold values from -6 to 6
- w_gate: bfloat16 [8192, 28672], P('col', 'row'), may hold values from -0.25 to 0.25
- w_up: bfloat16 [8192, 28672], P('col', 'row'), may hold values from -0.25 to 0.25
- w_down: bfloat16 [28672, 8192], P('row', 'col'), may hold values from -0.03125 to 0.03125
Outputs:
- grad_inputs: bfloat16 [512, 8192], P('row', 'col')
- grad_gate: bfloat16 [8192, 28672], P('col', 'row')
- grad_up: bfloat16 [8192, 28672], P('col', 'row')
- grad_down: bfloat16 [28672, 8192], P('row', 'col')
The draws below stay inside these ranges and needn't reach their ends.
All inputs are finite; a program needn't handle non-finite values.
Results may differ from the reference program's by a relative error of at most 0.005.
Values may be sent and summed in bfloat16 or wider, within the bound.
A program may use at most 128 MiB of HBM per device.

```python
import jax
import jax.numpy as jnp
from jax import lax

D = 8192
FF = 28672
TOKENS = 512


def level_of(rng, dims, shards, low, top_value):
    loudness, own = 1.0, jax.random.fold_in(rng, 6)
    for axis_at, parts in shards:
        heights = jnp.exp(jax.random.uniform(jax.random.fold_in(own, axis_at), (parts,), jnp.float32, low / len(shards), top_value / len(shards)))
        loudness = loudness * jnp.repeat(heights, dims[axis_at] // parts).reshape([-1 if axis == axis_at else 1 for axis in range(len(dims))])
    return loudness


def noise(rng, shape, scale, reach, split=(), held_as=jnp.bfloat16):
    gain = level_of(rng, shape, split, -0.22, 0.18) if split else 1.0
    array = jax.random.normal(rng, shape, jnp.float32) * scale * gain
    return jnp.minimum(jnp.maximum(array, -reach), reach).astype(held_as)


def setup_inputs(seed: int = 0) -> dict:
    streams_of = jax.random.split(jax.random.key(seed), 8)
    return {
        "inputs": noise(streams_of[0], (TOKENS, D), 1.0, 6.0, ((0, 8), (1, 16))),
        "grad_out": noise(streams_of[1], (TOKENS, D), 0.03, 0.1796875, ((0, 8), (1, 16))),
        "gate_pre": noise(streams_of[2], (TOKENS, FF), 1.0, 6.0, ((0, 16), (1, 8))),
        "up_pre": noise(streams_of[3], (TOKENS, FF), 1.0, 6.0, ((0, 16), (1, 8))),
        "w_gate": noise(streams_of[4], (D, FF), (D // 16) ** -0.5, 0.25, ((0, 16), (1, 8))),
        "w_up": noise(streams_of[5], (D, FF), (D // 16) ** -0.5, 0.25, ((0, 16), (1, 8))),
        "w_down": noise(streams_of[6], (FF, D), FF ** -0.5, 0.03125, ((0, 8), (1, 16))),
    }


def swiglu_back(gate_pre, up_pre, hidden_grad):
    gate_wide = gate_pre.astype(jnp.float32)
    up_wide = up_pre.astype(jnp.float32)
    logistic = jax.nn.sigmoid(gate_wide)
    swished = gate_wide * logistic
    hidden = (swished * up_wide).astype(jnp.bfloat16)
    up_grad = (hidden_grad * swished).astype(jnp.bfloat16)
    gate_grad = (hidden_grad * up_wide * logistic * (1.0 + gate_wide * (1.0 - logistic))).astype(jnp.bfloat16)
    return hidden, gate_grad, up_grad


def reference(inputs, grad_out, gate_pre, up_pre, w_gate, w_up, w_down):
    last_last = (((1,), (1,)), ((), ()))
    first_first = (((0,), (0,)), ((), ()))
    hidden_grad = lax.dot_general(grad_out, w_down, last_last, preferred_element_type=jnp.float32)
    hidden, gate_grad, up_grad = swiglu_back(gate_pre, up_pre, hidden_grad)
    grad_down = lax.dot_general(hidden, grad_out, first_first, preferred_element_type=jnp.float32).astype(jnp.bfloat16)
    grad_gate = lax.dot_general(inputs, gate_grad, first_first, preferred_element_type=jnp.float32).astype(jnp.bfloat16)
    grad_up = lax.dot_general(inputs, up_grad, first_first, preferred_element_type=jnp.float32).astype(jnp.bfloat16)
    grad_inputs = lax.dot_general(gate_grad, w_gate, last_last, preferred_element_type=jnp.float32)
    grad_inputs = grad_inputs + lax.dot_general(up_grad, w_up, last_last, preferred_element_type=jnp.float32)
    return grad_inputs.astype(jnp.bfloat16), grad_gate, grad_up, grad_down
```

```python
import jax
import jax.numpy as jnp
from jax import lax
from jax.experimental import pallas as pl
from jax.experimental.pallas import tpu as pltpu
from jax.sharding import PartitionSpec as P

MESH = pl.DeviceIdType.MESH
F32, BF16 = jnp.float32, jnp.bfloat16
NT = (((1,), (1,)), ((), ()))
TN = (((0,), (0,)), ((), ()))
R = 4
TB = 32
FFS = 3584
HALF = FFS // 2
QUART = FFS // 4
DS = 512
RB = 64
T2 = F32


def cols(h, q):
    return pl.ds(h * HALF + q * QUART, QUART)


def comm_kernel(
    inp_ref, go_ref, gp_ref, up_ref, wg_ref, wu_ref, wd_ref,
    hid_out, gg_out, ug_out, inp_out, go_out, gi_out,
    g_all, inp_all, go_all, gp, up, wg, wu, wd,
    p32, p16, r1, s1, m32, r2, s2, acc, sib, tot, zin, gi,
    loc, ss, rs,
):
    col, row = lax.axis_index("col"), lax.axis_index("row")
    y, x = col // R, lax.rem(col, R)
    z, core = row // 2, lax.rem(row, 2)

    def add(p, k):
        return lax.rem(p + k, R)

    def at(axis, k):
        return {"col": y * R + add(x, k)} if axis == "x" else {"col": add(y, k) * R + x}

    zdev = [{"row": add(z, k) * 2 + core} for k in (1, 2, 3)]
    other = {"row": z * 2 + 1 - core}

    def rc(k, src, dst, dev):
        return pltpu.make_async_remote_copy(
            src_ref=src, dst_ref=dst, send_sem=ss.at[k], recv_sem=rs.at[k], device_id=dev, device_id_type=MESH
        )

    def got(k, ref):
        rc(k, ref, ref, other).wait_recv()

    def sent(k, ref):
        rc(k, ref, ref, other).wait_send()

    def lc(k, src, dst):
        return pltpu.make_async_copy(src, dst, loc.at[k])

    loads = [
        lc(0, go_ref, go_all.at[row]), lc(1, gp_ref, gp), lc(2, up_ref, up), lc(3, wd_ref, wd),
        lc(4, inp_ref, inp_all.at[row]), lc(5, wg_ref, wg), lc(6, wu_ref, wu),
    ]
    for c in loads:
        c.start()

    barrier = pltpu.get_barrier_semaphore()
    peers = [at("x", 1), at("x", 3), at("y", 1), at("y", 3), other] + zdev
    for d in peers:
        pl.semaphore_signal(barrier, inc=1, device_id=d, device_id_type=MESH)
    pl.semaphore_wait(barrier, len(peers))

    class RowGather:
        def __init__(self, base, ref):
            self.b, self.ref = base, ref

        def start(self):
            for i in range(3):
                rc(self.b + i, self.ref.at[row], self.ref.at[row], zdev[i]).start()
            rc(self.b + 3, self.ref.at[row], self.ref.at[row], other).start()

        def src(self, i):
            return self.ref.at[add(z, 3 - i) * 2 + core]

        def forward(self):
            for i in range(3):
                got(self.b + i, self.src(i))
                rc(self.b + 4 + i, self.src(i), self.src(i), other).start()

        def finish(self):
            for i in range(3, 7):
                got(self.b + i, self.ref.at[row])
            for i in range(7):
                sent(self.b + i, self.ref.at[row])

    class Gather:
        def __init__(self, base, axis, view):
            self.b, self.axis, self.view = base, axis, view
            self.me = x if axis == "x" else y

        def start(self):
            b, v, me = self.b, self.view, self.me
            for k, q, step in ((0, 0, 1), (1, 1, 3), (2, 1, 1), (3, 0, 3)):
                rc(b + k, v(me, q), v(me, q), at(self.axis, step)).start()

        def forward(self):
            b, v, me = self.b, self.view, self.me
            got(b, v(add(me, 3), 0))
            rc(b + 4, v(add(me, 3), 0), v(add(me, 3), 0), at(self.axis, 1)).start()
            got(b + 1, v(add(me, 1), 1))
            rc(b + 5, v(add(me, 1), 1), v(add(me, 1), 1), at(self.axis, 3)).start()

        def near(self):
            got(self.b + 2, self.view(add(self.me, 3), 1))
            got(self.b + 3, self.view(add(self.me, 1), 0))

        def far(self):
            got(self.b + 4, self.view(add(self.me, 2), 0))
            got(self.b + 5, self.view(add(self.me, 2), 1))

        def drain(self):
            for k in range(6):
                sent(self.b + k, self.view(self.me, 0))

    def gathers(base, a, h):
        g = g_all.at[a]
        if h == 0:
            first = Gather(base, "x", lambda p, q: g.at[y, p, :, cols(h, q)])
            second = Gather(base + 6, "y", lambda p, q: g.at[p, :, :, cols(h, q)])
        else:
            first = Gather(base, "y", lambda p, q: g.at[p, x, :, cols(h, q)])
            second = Gather(base + 6, "x", lambda p, q: g.at[:, p, :, cols(h, q)])
        return first, second

    class Scatter:
        def __init__(self, base, axis, wide, narrow, recv, send):
            self.b, self.axis, self.wide, self.narrow, self.recv, self.send = base, axis, wide, narrow, recv, send
            self.me = x if axis == "x" else y

        def start(self):
            me = self.me
            for k, d, q, step in ((0, 2, 0, 1), (1, 2, 1, 3), (2, 1, 1, 1), (3, 3, 0, 3)):
                rc(self.b + k, self.narrow(add(me, d), q), self.recv.at[k], at(self.axis, step)).start()

        def forward(self):
            me = self.me
            for k, d, q, step in ((0, 1, 0, 1), (1, 3, 1, 3)):
                got(self.b + k, self.recv.at[k])
                part = self.wide(add(me, d), q)[...] + self.recv[k].astype(F32)
                self.send[k] = part.astype(self.send.dtype)
                rc(self.b + 4 + k, self.send.at[k], self.recv.at[4 + k], at(self.axis, step)).start()

        def result(self, q):
            k = (3, 4) if q == 0 else (2, 5)
            got(self.b + k[0], self.recv.at[k[0]])
            got(self.b + k[1], self.recv.at[k[1]])
            return self.wide(self.me, q)[...] + self.recv[k[0]].astype(F32) + self.recv[k[1]].astype(F32)

        def drain(self):
            for k in range(6):
                sent(self.b + k, self.recv.at[0])

    go_gather, inp_gather = RowGather(0, go_all), RowGather(7, inp_all)
    hid = [gathers(14 + 12 * h, 0, h) for h in range(2)]
    ggs = [gathers(38 + 12 * h, 1, h) for h in range(2)]
    ugs = [gathers(62 + 12 * h, 2, h) for h in range(2)]
    red1 = [
        Scatter(86, "y", lambda d, q: p32.at[d, :, :, cols(0, q)], lambda d, q: p16.at[d, :, :, cols(0, q)], r1.at[0], s1.at[0]),
        Scatter(92, "x", lambda d, q: p32.at[:, d, :, cols(1, q)], lambda d, q: p16.at[:, d, :, cols(1, q)], r1.at[1], s1.at[1]),
    ]
    red2 = [
        Scatter(98 + 6 * h, "xy"[h], lambda d, q, h=h: m32.at[h, q, d], lambda d, q, h=h: m32.at[h, q, d], r2.at[h], s2.at[h])
        for h in range(2)
    ]
    ROWSUM = 110

    loads[0].wait()
    go_gather.start()
    loads[4].wait()
    inp_gather.start()

    loads[1].wait()
    loads[2].wait()
    gw, uw = gp[...].astype(F32), up[...].astype(F32)
    g_all[0, y, x] = (gw * jax.nn.sigmoid(gw) * uw).astype(BF16)
    for f, s in hid:
        f.start()

    go_gather.forward()
    for f, s in hid:
        f.forward()
    go_gather.finish()
    loads[3].wait()

    def product(i, c):
        at_ = pl.ds(pl.multiple_of(i * 256, 256), 256)
        t = lax.dot_general(go_all[...].reshape(512, DS), wd[at_, :], NT, preferred_element_type=F32).reshape(R, R, TB, 256)
        p32[:, :, :, at_] = t
        p16[:, :, :, at_] = t.astype(BF16)
        return c

    lax.fori_loop(0, FFS // 256, product, 0)
    for r in red1:
        r.start()
    for f, s in hid:
        f.near()
        f.far()
    for r in red1:
        r.forward()
    for f, s in hid:
        s.start()
    inp_gather.forward()
    for h in range(2):
        for q in range(2):
            m32[h, q] = red1[h].result(q)
        red2[h].start()
    for h in range(2):
        red2[h].forward()
    for f, s in hid:
        s.forward()
    for h in range(2):
        for q in range(2):
            c = cols(h, q)
            hg = red2[h].result(q)
            gw, uw = gp[:, c].astype(F32), up[:, c].astype(F32)
            sg = jax.nn.sigmoid(gw)
            g_all[1, y, x, :, c] = (hg * uw * sg * (1.0 + gw * (1.0 - sg))).astype(BF16)
            g_all[2, y, x, :, c] = (hg * (gw * sg)).astype(BF16)
        ggs[h][0].start()
        ugs[h][0].start()
    for f, s in hid:
        s.near()
        s.far()
    save_h = lc(7, g_all.at[0], hid_out)
    save_h.start()
    for h in range(2):
        ggs[h][0].forward()
        ugs[h][0].forward()
    inp_gather.finish()
    save_i = lc(8, inp_all, inp_out)
    save_i.start()
    save_g = lc(9, go_all, go_out)
    save_g.start()
    for group in (ggs, ugs):
        for h in range(2):
            group[h][0].near()
            group[h][0].far()
            group[h][1].start()
    loads[5].wait()
    loads[6].wait()
    for group in (ggs, ugs):
        for h in range(2):
            group[h][1].forward()
    acc[...] = jnp.zeros_like(acc)

    def bundle(h, p):
        def piece(a, w):
            def body(i, t):
                c = pl.ds(pl.multiple_of(h * HALF + i * 256, 256), 256)
                lhs = g_all[a, p, :, :, c] if h == 0 else g_all[a, :, p, :, c]
                return t + lax.dot_general(lhs.reshape(R * TB, 256), w[:, c], NT, preferred_element_type=F32)

            return body

        t = jnp.zeros((R * TB, DS), F32)
        t = lax.fori_loop(0, HALF // 256, piece(1, wg), t)
        t = lax.fori_loop(0, HALF // 256, piece(2, wu), t).reshape(R, TB, DS)
        if h == 0:
            acc[p] += t
        else:
            acc[:, p] += t

    for h in range(2):
        bundle(h, (y, x)[h])
    for group in (ggs, ugs):
        for h in range(2):
            group[h][1].near()
    for h in range(2):
        for k in (1, 3):
            bundle(h, add((y, x)[h], k))
    for group in (ggs, ugs):
        for h in range(2):
            group[h][1].far()
    save_gg = lc(10, g_all.at[1], gg_out)
    save_gg.start()
    save_ug = lc(11, g_all.at[2], ug_out)
    save_ug.start()
    for h in range(2):
        bundle(h, add((y, x)[h], 2))

    rc(ROWSUM, acc.at[:, pl.ds(2 * (1 - core), 2)], sib, other).start()
    got(ROWSUM, sib)
    tot[...] = acc[:, pl.ds(2 * core, 2)] + sib[...]
    for i in range(3):
        rc(ROWSUM + 1 + i, tot.at[add(z, 1 + i)], zin.at[i], zdev[i]).start()
    total = tot[z]
    for i in range(3):
        got(ROWSUM + 1 + i, zin.at[i])
        total = total + zin[i]
    gi[...] = total.reshape(RB, DS).astype(BF16)
    save = lc(12, gi, gi_out)
    save.start()

    for group in (hid, ggs, ugs):
        for f, s in group:
            f.drain()
            s.drain()
    for r in red1 + red2:
        r.drain()
    sent(ROWSUM, sib)
    for i in range(3):
        sent(ROWSUM + 1 + i, zin.at[i])
    for c in (save_h, save_i, save_g, save_gg, save_ug, save):
        c.wait()


def weights_kernel(inp_ref, go_ref, hid_ref, gg_ref, ug_ref, dg_ref, du_ref, dd_ref):
    def rows(ref):
        return ref[...].reshape(512, ref.shape[-1])

    inp, go = rows(inp_ref), rows(go_ref)
    dg_ref[...] = lax.dot_general(inp, rows(gg_ref), TN, preferred_element_type=F32).astype(BF16)
    du_ref[...] = lax.dot_general(inp, rows(ug_ref), TN, preferred_element_type=F32).astype(BF16)
    dd_ref[...] = lax.dot_general(rows(hid_ref), go, TN, preferred_element_type=F32).astype(BF16)


def on_device(inputs, grad_out, gate_pre, up_pre, w_gate, w_up, w_down):
    anywhere = pl.BlockSpec(memory_space=pl.ANY)
    block = jax.ShapeDtypeStruct((R, R, TB, FFS), BF16)
    tokens = jax.ShapeDtypeStruct((2 * R, RB, DS), BF16)
    hidden, gate_grad, up_grad, inp_all, go_all, grad_inputs = pl.pallas_call(
        comm_kernel,
        out_shape=(block, block, block, tokens, tokens, jax.ShapeDtypeStruct((RB, DS), BF16)),
        in_specs=[anywhere] * 7,
        out_specs=[anywhere] * 6,
        scratch_shapes=[
            pltpu.VMEM((3, R, R, TB, FFS), BF16),
            pltpu.VMEM((2 * R, RB, DS), BF16),
            pltpu.VMEM((2 * R, RB, DS), BF16),
            pltpu.VMEM((TB, FFS), BF16),
            pltpu.VMEM((TB, FFS), BF16),
            pltpu.VMEM((DS, FFS), BF16),
            pltpu.VMEM((DS, FFS), BF16),
            pltpu.VMEM((FFS, DS), BF16),
            pltpu.VMEM((R, R, TB, FFS), F32),
            pltpu.VMEM((R, R, TB, FFS), BF16),
            pltpu.VMEM((2, 6, R, TB, QUART), BF16),
            pltpu.VMEM((2, 2, R, TB, QUART), BF16),
            pltpu.VMEM((2, 2, R, TB, QUART), F32),
            pltpu.VMEM((2, 6, TB, QUART), T2),
            pltpu.VMEM((2, 2, TB, QUART), T2),
            pltpu.VMEM((R, R, TB, DS), F32),
            pltpu.VMEM((R, 2, TB, DS), F32),
            pltpu.VMEM((R, 2, TB, DS), F32),
            pltpu.VMEM((3, 2, TB, DS), F32),
            pltpu.VMEM((RB, DS), BF16),
            pltpu.SemaphoreType.DMA((13,)),
            pltpu.SemaphoreType.DMA((114,)),
            pltpu.SemaphoreType.DMA((114,)),
        ],
        compiler_params=pltpu.CompilerParams(
            collective_id=0, has_side_effects=True, vmem_limit_bytes=60 * 1024 * 1024
        ),
    )(inputs, grad_out, gate_pre, up_pre, w_gate, w_up, w_down)

    tile = 512
    wide = pl.BlockSpec((R, R, TB, tile), lambda i: (0, 0, 0, i))
    whole = pl.BlockSpec((2 * R, RB, DS), lambda i: (0, 0, 0))
    grad_gate, grad_up, grad_down = pl.pallas_call(
        weights_kernel,
        grid=(FFS // tile,),
        out_shape=(
            jax.ShapeDtypeStruct((DS, FFS), BF16),
            jax.ShapeDtypeStruct((DS, FFS), BF16),
            jax.ShapeDtypeStruct((FFS, DS), BF16),
        ),
        in_specs=[whole, whole, wide, wide, wide],
        out_specs=[
            pl.BlockSpec((DS, tile), lambda i: (0, i)),
            pl.BlockSpec((DS, tile), lambda i: (0, i)),
            pl.BlockSpec((tile, DS), lambda i: (i, 0)),
        ],
        compiler_params=pltpu.CompilerParams(vmem_limit_bytes=48 * 1024 * 1024),
    )(inp_all, go_all, hidden, gate_grad, up_grad)
    return (grad_inputs, grad_gate, grad_up, grad_down)


def solution(mesh):
    placed = (
        P("row", "col"),
        P("row", "col"),
        P("col", "row"),
        P("col", "row"),
        P("col", "row"),
        P("col", "row"),
        P("row", "col"),
    )
    return jax.shard_map(
        on_device,
        mesh=mesh,
        in_specs=placed,
        out_specs=(P("row", "col"), P("col", "row"), P("col", "row"), P("row", "col")),
        check_vma=False,
    )
```

```python
import jax
import jax.numpy as jnp
from jax import lax
from jax.experimental import pallas as pl
from jax.experimental.pallas import tpu as pltpu
from jax.sharding import PartitionSpec as P

MESH = pl.DeviceIdType.MESH
F32, BF16 = jnp.float32, jnp.bfloat16
NT = (((1,), (1,)), ((), ()))
TN = (((0,), (0,)), ((), ()))
R = 4
TB = 32
FFS = 3584
HALF = FFS // 2
QR = TB // 2
DS = 512
RB = 64
T2 = F32


CHUNKS = (4, 4, 3, 3)
LAG = 1
HIDDEN = (0, 1, 4, 7)


def comm_kernel(
    inp_ref, go_ref, gp_ref, up_ref, wg_ref, wu_ref, wd_ref,
    hid_all, g_all, inp_all, go_all, own, to1, to2, to3,
    gp, up, wg, wu, wd,
    p32, p16, r1, s1, m32, r2, s2, acc, sib,
    loc, ss, rs,
):
    col, row = lax.axis_index("col"), lax.axis_index("row")
    y, x = col // R, lax.rem(col, R)
    z, core = row // 2, lax.rem(row, 2)
    sems = [0]

    def take(n):
        sems[0] += n
        return sems[0] - n

    def add(p, k):
        return lax.rem(p + k, R)

    def at(axis, k):
        return {"col": y * R + add(x, k)} if axis == "x" else {"col": add(y, k) * R + x}

    zdev = [{"row": add(z, k) * 2 + core} for k in (1, 2, 3)]
    other = {"row": z * 2 + 1 - core}

    def rc(k, src, dst, dev):
        return pltpu.make_async_remote_copy(
            src_ref=src, dst_ref=dst, send_sem=ss.at[k], recv_sem=rs.at[k], device_id=dev, device_id_type=MESH
        )

    def got(k, ref):
        rc(k, ref, ref, other).wait_recv()

    def sent(k, ref):
        rc(k, ref, ref, other).wait_send()

    def lc(k, src, dst):
        return pltpu.make_async_copy(src, dst, loc.at[k])

    loads = [
        lc(0, go_ref, go_all.at[row]), lc(1, gp_ref, gp), lc(2, up_ref, up), lc(3, wd_ref, wd),
        lc(4, inp_ref, inp_all.at[row]), lc(5, wg_ref, wg), lc(6, wu_ref, wu),
    ]
    for c in loads:
        c.start()

    barrier = pltpu.get_barrier_semaphore()
    peers = [at("x", 1), at("x", 3), at("y", 1), at("y", 3), other] + zdev
    for d in peers:
        pl.semaphore_signal(barrier, inc=1, device_id=d, device_id_type=MESH)
    pl.semaphore_wait(barrier, len(peers))

    class RowGather:
        def __init__(self, ref):
            self.b, self.ref = take(7), ref

        def start(self):
            for i in range(3):
                rc(self.b + i, self.ref.at[row], self.ref.at[row], zdev[i]).start()
            rc(self.b + 3, self.ref.at[row], self.ref.at[row], other).start()

        def src(self, i):
            return self.ref.at[add(z, 3 - i) * 2 + core]

        def forward(self):
            for i in range(3):
                got(self.b + i, self.src(i))
                rc(self.b + 4 + i, self.src(i), self.src(i), other).start()

        def finish(self):
            for i in range(3, 7):
                got(self.b + i, self.ref.at[row])
            for i in range(7):
                sent(self.b + i, self.ref.at[row])

    class Gather:
        def __init__(self, axis, view):
            self.b, self.axis, self.view = take(6), axis, view
            self.me = x if axis == "x" else y

        def start(self):
            b, v, me = self.b, self.view, self.me
            for k, q, step in ((0, 0, 1), (1, 1, 3), (2, 1, 1), (3, 0, 3)):
                rc(b + k, v(me, q), v(me, q), at(self.axis, step)).start()

        def forward(self):
            b, v, me = self.b, self.view, self.me
            got(b, v(add(me, 3), 0))
            rc(b + 4, v(add(me, 3), 0), v(add(me, 3), 0), at(self.axis, 1)).start()
            got(b + 1, v(add(me, 1), 1))
            rc(b + 5, v(add(me, 1), 1), v(add(me, 1), 1), at(self.axis, 3)).start()

        def rest(self):
            got(self.b + 2, self.view(add(self.me, 3), 1))
            got(self.b + 3, self.view(add(self.me, 1), 0))
            got(self.b + 4, self.view(add(self.me, 2), 0))
            got(self.b + 5, self.view(add(self.me, 2), 1))

        def drain(self):
            for k in range(6):
                sent(self.b + k, self.view(self.me, 0))

    class Scatter:
        def __init__(self, axis, wide, narrow, recv, send):
            self.b, self.axis, self.wide, self.narrow, self.recv, self.send = take(6), axis, wide, narrow, recv, send
            self.me = x if axis == "x" else y

        def start(self):
            me = self.me
            for k, d, q, step in ((0, 2, 0, 1), (1, 2, 1, 3), (2, 1, 1, 1), (3, 3, 0, 3)):
                rc(self.b + k, self.narrow(add(me, d), q), self.recv(k), at(self.axis, step)).start()

        def forward(self):
            me = self.me
            for k, d, q, step in ((0, 1, 0, 1), (1, 3, 1, 3)):
                got(self.b + k, self.recv(k))
                part = self.wide(add(me, d), q)[...] + self.recv(k)[...].astype(F32)
                self.send(k)[...] = part.astype(self.send(k).dtype)
                rc(self.b + 4 + k, self.send(k), self.recv(4 + k), at(self.axis, step)).start()

        def result(self, q):
            i, k = (3, 4) if q == 0 else (2, 5)
            got(self.b + i, self.recv(i))
            got(self.b + k, self.recv(k))
            return self.wide(self.me, q)[...] + self.recv(i)[...].astype(F32) + self.recv(k)[...].astype(F32)

        def drain(self):
            for k in range(6):
                sent(self.b + k, self.recv(0))

    def gathers(c, h, one):
        if h == 0:
            return Gather("x", lambda p, q: one(y, p, q, c)), Gather("y", lambda p, q: one(p, slice(None), q, c))
        return Gather("y", lambda p, q: one(p, x, q, c)), Gather("x", lambda p, q: one(slice(None), p, q, c))

    def rows(q):
        return pl.ds(q * QR, QR)

    class Chunk:
        def __init__(self, j):
            self.w = CHUNKS[j] * 128
            self.o, self.ho = 256 * sum(CHUNKS[:j]), 128 * sum(CHUNKS[:j])
            self.red1, self.red2, self.gat = [], [], []
            hc = pl.ds(self.ho, self.w)
            for h in range(2):
                c = self.cols(h)
                pick = (lambda ref, d, q, c=c: ref.at[d, :, rows(q), c]) if h == 0 else (
                    lambda ref, d, q, c=c: ref.at[:, d, rows(q), c])
                self.red1.append(Scatter(
                    "yx"[h], lambda d, q, f=pick: f(p32, d, q), lambda d, q, f=pick: f(p16, d, q),
                    lambda k, h=h: r1.at[h, k, :, :, hc], lambda k, h=h: s1.at[h, k, :, :, hc]))
                part = lambda d, q, h=h: m32.at[h, d, rows(q), hc]
                self.red2.append(Scatter(
                    "xy"[h], part, part, lambda k, h=h: r2.at[h, k, :, hc], lambda k, h=h: s2.at[h, k, :, hc]))
                self.gat.append(gathers(c, h, lambda a, b, q, c: g_all.at[:, a, b, rows(q), c]))
            self.hc = hc

        def cols(self, h):
            return pl.ds(self.o + h * self.w, self.w)

        def product(self):
            def body(i, t):
                c = pl.ds(pl.multiple_of(self.o + i * 256, 256), 256)
                v = lax.dot_general(
                    go_all[...].reshape(512, DS), wd[c, :], NT, preferred_element_type=F32
                ).reshape(R, R, TB, 256)
                p32[:, :, :, c] = v
                p16[:, :, :, c] = v.astype(BF16)
                return t

            lax.fori_loop(0, self.w // 128, body, 0)

        def step(self, s):
            for h in range(2):
                if s == 0:
                    if h == 0:
                        self.product()
                    self.red1[h].start()
                if s == 1:
                    self.red1[h].forward()
                if s == 2:
                    for q in range(2):
                        m32[h, :, rows(q), self.hc] = self.red1[h].result(q)
                    self.red2[h].start()
                if s == 3:
                    self.red2[h].forward()
                if s == 4:
                    c = self.cols(h)
                    for q in range(2):
                        hg = self.red2[h].result(q)
                        gw, uw = gp[rows(q), c].astype(F32), up[rows(q), c].astype(F32)
                        sg = jax.nn.sigmoid(gw)
                        g_all[0, y, x, rows(q), c] = (hg * uw * sg * (1.0 + gw * (1.0 - sg))).astype(BF16)
                        g_all[1, y, x, rows(q), c] = (hg * (gw * sg)).astype(BF16)
                    self.gat[h][0].start()
                if s == 5:
                    self.gat[h][0].forward()
                if s == 6:
                    self.gat[h][0].rest()
                    self.gat[h][1].start()
                if s == 7:
                    self.gat[h][1].forward()
                if s == 8:
                    self.gat[h][1].rest()
            if s == 8:
                c = pl.ds(self.o, 2 * self.w)
                for a, w in ((0, wg), (1, wu)):
                    lhs = g_all[a, :, :, :, c].reshape(512, 2 * self.w)
                    acc[...] += lax.dot_general(
                        lhs, w[:, c], NT, preferred_element_type=F32).reshape(R, R, TB, DS)

        def drain(self):
            for h in range(2):
                for t in (self.red1[h], self.red2[h], *self.gat[h]):
                    t.drain()

    go_gather, inp_gather = RowGather(go_all), RowGather(inp_all)
    hid = [gathers(pl.ds(h * HALF, HALF), h, lambda a, b, q, c: hid_all.at[a, b, rows(q), c]) for h in range(2)]
    chunks = [Chunk(j) for j in range(len(CHUNKS))]
    rowsum = take(1)

    loads[0].wait()
    go_gather.start()
    loads[4].wait()
    inp_gather.start()

    loads[1].wait()
    loads[2].wait()
    gw, uw = gp[...].astype(F32), up[...].astype(F32)
    hid_all[y, x] = (gw * jax.nn.sigmoid(gw) * uw).astype(BF16)
    for f, s in hid:
        f.start()
    acc[...] = jnp.zeros_like(acc)
    go_gather.forward()
    go_gather.finish()
    for c in loads[3:4] + loads[5:]:
        c.wait()

    for t in range(9 + LAG * (len(CHUNKS) - 1)):
        for j, chunk in enumerate(chunks):
            if 0 <= t - LAG * j <= 8:
                chunk.step(t - LAG * j)
        if t == 0:
            inp_gather.forward()
        for f, s in hid:
            if t == HIDDEN[0]:
                f.forward()
            if t == HIDDEN[1]:
                f.rest()
                s.start()
            if t == HIDDEN[2]:
                s.forward()
            if t == HIDDEN[3]:
                s.rest()

    rc(rowsum, acc.at[:, pl.ds(2 * (1 - core), 2)], sib, other).start()
    inp_gather.finish()
    for f, s in hid:
        f.drain()
        s.drain()
    for chunk in chunks:
        chunk.drain()
    got(rowsum, sib)
    for i, ref in enumerate((own, to1, to2, to3)):
        p = add(z, i)
        ref[...] = (acc[p, pl.ds(2 * core, 2)] + sib[p]).reshape(RB, DS)
    sent(rowsum, sib)


WT = 512


def weights_kernel(inp_ref, go_ref, hid_ref, g_ref, dg_ref, du_ref, dd_ref, dg, du, dd, sem):
    inp, go = inp_ref[...].reshape(512, DS), go_ref[...].reshape(512, DS)

    def outs(i):
        c = pl.ds(pl.multiple_of(i * WT, WT), WT)
        k = lax.rem(i, 2)
        return (
            pltpu.make_async_copy(dg.at[k], dg_ref.at[:, c], sem.at[0, k]),
            pltpu.make_async_copy(du.at[k], du_ref.at[:, c], sem.at[1, k]),
            pltpu.make_async_copy(dd.at[k], dd_ref.at[c, :], sem.at[2, k]),
        )

    def body(i, t):
        c = pl.ds(pl.multiple_of(i * WT, WT), WT)
        k = lax.rem(i, 2)

        @pl.when(i >= 2)
        def _():
            for o in outs(i - 2):
                o.wait()

        a, b, d = outs(i)
        dg[k] = lax.dot_general(inp, g_ref[0, :, :, :, c].reshape(512, WT), TN, preferred_element_type=F32).astype(BF16)
        a.start()
        du[k] = lax.dot_general(inp, g_ref[1, :, :, :, c].reshape(512, WT), TN, preferred_element_type=F32).astype(BF16)
        b.start()
        dd[k] = lax.dot_general(hid_ref[:, :, :, c].reshape(512, WT), go, TN, preferred_element_type=F32).astype(BF16)
        d.start()
        return t

    n = FFS // WT
    lax.fori_loop(0, n, body, 0)
    for i in (n - 2, n - 1):
        for o in outs(i):
            o.wait()


def on_device(inputs, grad_out, gate_pre, up_pre, w_gate, w_up, w_down):
    anywhere = pl.BlockSpec(memory_space=pl.ANY)
    vmem = pl.BlockSpec(memory_space=pltpu.VMEM)
    tokens = pltpu.VMEM((2 * R, RB, DS), BF16)
    share = pltpu.VMEM((RB, DS), F32)
    nsem = 14 + 24 + 48 * len(CHUNKS) + 1
    hidden, grads, inp_all, go_all, own, to1, to2, to3 = pl.pallas_call(
        comm_kernel,
        out_shape=(
            pltpu.VMEM((R, R, TB, FFS), BF16), pltpu.VMEM((2, R, R, TB, FFS), BF16), tokens, tokens,
            share, share, share, share,
        ),
        in_specs=[anywhere] * 7,
        out_specs=[vmem] * 8,
        scratch_shapes=[
            pltpu.VMEM((TB, FFS), BF16),
            pltpu.VMEM((TB, FFS), BF16),
            pltpu.VMEM((DS, FFS), BF16),
            pltpu.VMEM((DS, FFS), BF16),
            pltpu.VMEM((FFS, DS), BF16),
            pltpu.VMEM((R, R, TB, FFS), F32),
            pltpu.VMEM((R, R, TB, FFS), BF16),
            pltpu.VMEM((2, 6, R, QR, HALF), BF16),
            pltpu.VMEM((2, 2, R, QR, HALF), BF16),
            pltpu.VMEM((2, R, TB, HALF), F32),
            pltpu.VMEM((2, 6, QR, HALF), T2),
            pltpu.VMEM((2, 2, QR, HALF), T2),
            pltpu.VMEM((R, R, TB, DS), F32),
            pltpu.VMEM((R, 2, TB, DS), F32),
            pltpu.SemaphoreType.DMA((7,)),
            pltpu.SemaphoreType.DMA((nsem,)),
            pltpu.SemaphoreType.DMA((nsem,)),
        ],
        compiler_params=pltpu.CompilerParams(
            collective_id=0, has_side_effects=True, vmem_limit_bytes=46 * 1024 * 1024
        ),
    )(inputs, grad_out, gate_pre, up_pre, w_gate, w_up, w_down)

    moved = [
        lax.ppermute(v, "row", [(d, (d + 2 * k) % (2 * R)) for d in range(2 * R)])
        for k, v in ((1, to1), (2, to2), (3, to3))
    ]
    grad_gate, grad_up, grad_down = pl.pallas_call(
        weights_kernel,
        out_shape=(
            jax.ShapeDtypeStruct((DS, FFS), BF16),
            jax.ShapeDtypeStruct((DS, FFS), BF16),
            jax.ShapeDtypeStruct((FFS, DS), BF16),
        ),
        in_specs=[vmem] * 4,
        out_specs=[anywhere] * 3,
        scratch_shapes=[
            pltpu.VMEM((2, DS, WT), BF16),
            pltpu.VMEM((2, DS, WT), BF16),
            pltpu.VMEM((2, WT, DS), BF16),
            pltpu.SemaphoreType.DMA((3, 2)),
        ],
        cost_estimate=pl.CostEstimate(flops=6 * 512 * DS * FFS, bytes_accessed=12 * DS * FFS, transcendentals=0),
        compiler_params=pltpu.CompilerParams(vmem_limit_bytes=32 * 1024 * 1024),
    )(inp_all, go_all, hidden, grads)
    grad_inputs = (own + moved[0] + moved[1] + moved[2]).astype(BF16)
    return (grad_inputs, grad_gate, grad_up, grad_down)


def solution(mesh):
    placed = (
        P("row", "col"),
        P("row", "col"),
        P("col", "row"),
        P("col", "row"),
        P("col", "row"),
        P("col", "row"),
        P("row", "col"),
    )
    return jax.shard_map(
        on_device,
        mesh=mesh,
        in_specs=placed,
        out_specs=(P("row", "col"), P("col", "row"), P("col", "row"), P("row", "col")),
        check_vma=False,
    )
```

```python
import jax
import jax.numpy as jnp
from jax import lax
from jax.experimental import pallas as pl
from jax.experimental.pallas import tpu as pltpu
from jax.sharding import PartitionSpec as P

MESH = pl.DeviceIdType.MESH
F32, BF16 = jnp.float32, jnp.bfloat16
NT = (((1,), (1,)), ((), ()))
TN = (((0,), (0,)), ((), ()))
R = 4
TB = 32
FFS = 3584
HALF = FFS // 2
QR = TB // 2
DS = 512
RB = 64


CHUNKS = (4, 4, 4, 2)
FAR = 2
LAG = 1


def comm_kernel(
    inp_ref, go_ref, gp_ref, up_ref, wg_ref, wu_ref, wd_ref,
    hid_all, g_all, inp_all, go_all, gi,
    gp, up, wg, wu, wd,
    p32, p16, r1, s1, m32, m16, r2, s2, acc, sib, zout, zin,
    loc, ss, rs,
):
    col, row = lax.axis_index("col"), lax.axis_index("row")
    y, x = col // R, lax.rem(col, R)
    z, core = row // 2, lax.rem(row, 2)
    sems = [0]

    def take(n):
        sems[0] += n
        return sems[0] - n

    def add(p, k):
        return lax.rem(p + k, R)

    def at(axis, k):
        return {"col": y * R + add(x, k)} if axis == "x" else {"col": add(y, k) * R + x}

    zdev = [{"row": add(z, k) * 2 + core} for k in (1, 2, 3)]
    other = {"row": z * 2 + 1 - core}

    def rc(k, src, dst, dev):
        return pltpu.make_async_remote_copy(
            src_ref=src, dst_ref=dst, send_sem=ss.at[k], recv_sem=rs.at[k], device_id=dev, device_id_type=MESH
        )

    def got(k, ref):
        rc(k, ref, ref, other).wait_recv()

    def sent(k, ref):
        rc(k, ref, ref, other).wait_send()

    def lc(k, src, dst):
        return pltpu.make_async_copy(src, dst, loc.at[k])

    loads = [
        lc(0, go_ref, go_all.at[row]), lc(1, gp_ref, gp), lc(2, up_ref, up), lc(3, wd_ref, wd),
        lc(4, inp_ref, inp_all.at[row]), lc(5, wg_ref, wg), lc(6, wu_ref, wu),
    ]
    for c in loads:
        c.start()

    barrier = pltpu.get_barrier_semaphore()
    peers = [at("x", 1), at("x", 3), at("y", 1), at("y", 3), other] + zdev
    for d in peers:
        pl.semaphore_signal(barrier, inc=1, device_id=d, device_id_type=MESH)
    pl.semaphore_wait(barrier, len(peers))

    class RowGather:
        def __init__(self, ref):
            self.b, self.ref = take(7), ref

        def start(self):
            for i in range(3):
                rc(self.b + i, self.ref.at[row], self.ref.at[row], zdev[i]).start()
            rc(self.b + 3, self.ref.at[row], self.ref.at[row], other).start()

        def src(self, i):
            return self.ref.at[add(z, 3 - i) * 2 + core]

        def forward(self):
            for i in range(3):
                got(self.b + i, self.src(i))
                rc(self.b + 4 + i, self.src(i), self.src(i), other).start()

        def finish(self):
            for i in range(3, 7):
                got(self.b + i, self.ref.at[row])
            for i in range(7):
                sent(self.b + i, self.ref.at[row])

    class Gather:
        def __init__(self, axis, view):
            self.b, self.axis, self.view = take(6), axis, view
            self.me = x if axis == "x" else y

        def start(self):
            b, v, me = self.b, self.view, self.me
            for k, q, step in ((0, 0, 1), (1, 1, 3), (2, 1, 1), (3, 0, 3)):
                rc(b + k, v(me, q), v(me, q), at(self.axis, step)).start()

        def forward(self):
            b, v, me = self.b, self.view, self.me
            got(b, v(add(me, 3), 0))
            rc(b + 4, v(add(me, 3), 0), v(add(me, 3), 0), at(self.axis, 1)).start()
            got(b + 1, v(add(me, 1), 1))
            rc(b + 5, v(add(me, 1), 1), v(add(me, 1), 1), at(self.axis, 3)).start()

        def near(self):
            got(self.b + 2, self.view(add(self.me, 3), 1))
            got(self.b + 3, self.view(add(self.me, 1), 0))

        def far(self):
            got(self.b + 4, self.view(add(self.me, 2), 0))
            got(self.b + 5, self.view(add(self.me, 2), 1))

        def drain(self):
            for k in range(6):
                sent(self.b + k, self.view(self.me, 0))

    class Scatter:
        def __init__(self, axis, wide, narrow, recv, send):
            self.b, self.axis, self.wide, self.narrow, self.recv, self.send = take(6), axis, wide, narrow, recv, send
            self.me = x if axis == "x" else y

        def start(self):
            me = self.me
            for k, d, q, step in ((0, 2, 0, 1), (1, 2, 1, 3), (2, 1, 1, 1), (3, 3, 0, 3)):
                rc(self.b + k, self.narrow(add(me, d), q), self.recv(k), at(self.axis, step)).start()

        def forward(self):
            me = self.me
            for k, d, q, step in ((0, 1, 0, 1), (1, 3, 1, 3)):
                got(self.b + k, self.recv(k))
                part = self.wide(add(me, d), q)[...] + self.recv(k)[...].astype(F32)
                self.send(k)[...] = part.astype(self.send(k).dtype)
                rc(self.b + 4 + k, self.send(k), self.recv(4 + k), at(self.axis, step)).start()

        def result(self, q):
            i, k = (3, 4) if q == 0 else (2, 5)
            got(self.b + i, self.recv(i))
            got(self.b + k, self.recv(k))
            return self.wide(self.me, q)[...] + self.recv(i)[...].astype(F32) + self.recv(k)[...].astype(F32)

        def drain(self):
            for k in range(6):
                sent(self.b + k, self.recv(0))

    def gathers(c, h, one):
        if h == 0:
            return Gather("x", lambda p, q: one(y, p, q, c)), Gather("y", lambda p, q: one(p, slice(None), q, c))
        return Gather("y", lambda p, q: one(p, x, q, c)), Gather("x", lambda p, q: one(slice(None), p, q, c))

    def rows(q):
        return pl.ds(q * QR, QR)

    class Chunk:
        def __init__(self, j):
            self.w = CHUNKS[j] * 128
            self.o, self.ho = 256 * sum(CHUNKS[:j]), 128 * sum(CHUNKS[:j])
            self.red1, self.red2, self.gat = [], [], []
            hc = pl.ds(self.ho, self.w)
            for h in range(2):
                c = self.cols(h)
                pick = (lambda ref, d, q, c=c: ref.at[d, :, rows(q), c]) if h == 0 else (
                    lambda ref, d, q, c=c: ref.at[:, d, rows(q), c])
                self.red1.append(Scatter(
                    "yx"[h], lambda d, q, f=pick: f(p32, d, q), lambda d, q, f=pick: f(p16, d, q),
                    lambda k, h=h: r1.at[h, k, :, :, hc], lambda k, h=h: s1.at[h, k, :, :, hc]))
                self.red2.append(Scatter(
                    "xy"[h], lambda d, q, h=h: m32.at[h, d, rows(q), hc], lambda d, q, h=h: m16.at[h, d, rows(q), hc],
                    lambda k, h=h: r2.at[h, k, :, hc], lambda k, h=h: s2.at[h, k, :, hc]))
                self.gat.append(gathers(c, h, lambda a, b, q, c: g_all.at[:, a, b, rows(q), c]))
            self.hc = hc

        def cols(self, h):
            return pl.ds(self.o + h * self.w, self.w)

        def product(self):
            def body(i, t):
                c = pl.ds(pl.multiple_of(self.o + i * 256, 256), 256)
                v = lax.dot_general(
                    go_all[...].reshape(512, DS), wd[c, :], NT, preferred_element_type=F32
                ).reshape(R, R, TB, 256)
                p32[:, :, :, c] = v
                p16[:, :, :, c] = v.astype(BF16)
                return t

            lax.fori_loop(0, self.w // 128, body, 0)

        def step(self, s):
            for h in range(2):
                if s == 0:
                    if h == 0:
                        self.product()
                    self.red1[h].start()
                if s == 1:
                    self.red1[h].forward()
                if s == 2:
                    for q in range(2):
                        v = self.red1[h].result(q)
                        m32[h, :, rows(q), self.hc] = v
                        m16[h, :, rows(q), self.hc] = v.astype(BF16)
                    self.red2[h].start()
                if s == 3:
                    self.red2[h].forward()
                if s == 4:
                    c = self.cols(h)
                    for q in range(2):
                        hg = self.red2[h].result(q)
                        gw, uw = gp[rows(q), c].astype(F32), up[rows(q), c].astype(F32)
                        sg = jax.nn.sigmoid(gw)
                        g_all[0, y, x, rows(q), c] = (hg * uw * sg * (1.0 + gw * (1.0 - sg))).astype(BF16)
                        g_all[1, y, x, rows(q), c] = (hg * (gw * sg)).astype(BF16)
                    self.gat[h][0].start()
                if s == 5:
                    self.gat[h][0].forward()
                if s == 6:
                    self.gat[h][0].near()
                    self.gat[h][0].far()
                    self.gat[h][1].start()
                if s == 7:
                    self.gat[h][1].forward()
                if s == 8:
                    self.gat[h][1].near()
                    self.gat[h][1].far()
            if s == 9:
                c = pl.ds(self.o, 2 * self.w)
                for a, w in ((0, wg), (1, wu)):
                    lhs = g_all[a, :, :, :, c].reshape(512, 2 * self.w)
                    acc[...] += lax.dot_general(
                        lhs, w[:, c], NT, preferred_element_type=F32).reshape(R, R, TB, DS)

        def drain(self):
            for h in range(2):
                for t in (self.red1[h], self.red2[h], *self.gat[h]):
                    t.drain()

    go_gather, inp_gather = RowGather(go_all), RowGather(inp_all)
    hid = []
    for h in range(2):
        view = lambda a, b, q, h=h: hid_all.at[a, b, rows(q), pl.ds(h * HALF, HALF)]
        if h == 0:
            hid.append((Gather("x", lambda p, q, v=view: v(y, p, q)), [
                Gather("y", lambda p, q, v=view, k=k: v(p, add(x, k), q)) for k in range(R)]))
        else:
            hid.append((Gather("y", lambda p, q, v=view: v(p, x, q)), [
                Gather("x", lambda p, q, v=view, k=k: v(add(y, k), p, q)) for k in range(R)]))
    chunks = [Chunk(j) for j in range(len(CHUNKS))]
    rowsum = take(4)

    loads[0].wait()
    go_gather.start()
    loads[4].wait()
    inp_gather.start()

    loads[1].wait()
    loads[2].wait()
    gw, uw = gp[...].astype(F32), up[...].astype(F32)
    hid_all[y, x] = (gw * jax.nn.sigmoid(gw) * uw).astype(BF16)
    for f, s in hid:
        f.start()
        s[0].start()
    acc[...] = jnp.zeros_like(acc)
    for f, s in hid:
        f.forward()
        f.near()
        s[1].start()
        s[3].start()
    go_gather.forward()
    go_gather.finish()
    for c in loads[3:4] + loads[5:]:
        c.wait()

    last = 8 + LAG * (len(CHUNKS) - 1)
    for t in range(last + 1):
        for j, chunk in enumerate(chunks):
            if 0 <= t - LAG * j <= 8:
                chunk.step(t - LAG * j)
            if t - LAG * j == 8 and t < last:
                chunk.step(9)
        if t == 0:
            inp_gather.forward()
        for f, s in hid:
            if t == last - FAR:
                f.far()
                s[2].start()
            if t == last - 1:
                for k in (0, 1, 3):
                    s[k].forward()
            if t == last:
                s[2].forward()
    chunks[-1].step(9)

    rc(rowsum, acc.at[:, pl.ds(2 * (1 - core), 2)], sib, other).start()
    inp_gather.finish()
    for chunk in chunks:
        chunk.drain()
    got(rowsum, sib)
    for i in range(3):
        p = add(z, i + 1)
        zout[i] = (acc[p, pl.ds(2 * core, 2)] + sib[p]).reshape(RB, DS).astype(BF16)
        rc(rowsum + 1 + i, zout.at[i], zin.at[i], zdev[i]).start()
    total = (acc[z, pl.ds(2 * core, 2)] + sib[z]).reshape(RB, DS)
    for f, s in hid:
        for g in s:
            g.near()
            g.far()
        for g in [f] + s:
            g.drain()
    for i in range(3):
        got(rowsum + 1 + i, zin.at[i])
        total = total + zin[i].astype(F32)
    gi[...] = total.astype(BF16)
    sent(rowsum, sib)
    for i in range(3):
        sent(rowsum + 1 + i, zout.at[i])


WT = 512


def weights_kernel(inp_ref, go_ref, hid_ref, g_ref, gi_ref, gi_out, dg_ref, du_ref, dd_ref, dg, du, dd, sem, one):
    save = pltpu.make_async_copy(gi_ref, gi_out, one)
    save.start()
    inp, go = inp_ref[...].reshape(512, DS), go_ref[...].reshape(512, DS)

    def outs(i):
        c = pl.ds(pl.multiple_of(i * WT, WT), WT)
        k = lax.rem(i, 2)
        return (
            pltpu.make_async_copy(dg.at[k], dg_ref.at[:, c], sem.at[0, k]),
            pltpu.make_async_copy(du.at[k], du_ref.at[:, c], sem.at[1, k]),
            pltpu.make_async_copy(dd.at[k], dd_ref.at[c, :], sem.at[2, k]),
        )

    def body(i, t):
        c = pl.ds(pl.multiple_of(i * WT, WT), WT)
        k = lax.rem(i, 2)

        @pl.when(i >= 2)
        def _():
            for o in outs(i - 2):
                o.wait()

        a, b, d = outs(i)
        dg[k] = lax.dot_general(inp, g_ref[0, :, :, :, c].reshape(512, WT), TN, preferred_element_type=F32).astype(BF16)
        a.start()
        du[k] = lax.dot_general(inp, g_ref[1, :, :, :, c].reshape(512, WT), TN, preferred_element_type=F32).astype(BF16)
        b.start()
        dd[k] = lax.dot_general(hid_ref[:, :, :, c].reshape(512, WT), go, TN, preferred_element_type=F32).astype(BF16)
        d.start()
        return t

    n = FFS // WT
    lax.fori_loop(0, n, body, 0)
    for i in (n - 2, n - 1):
        for o in outs(i):
            o.wait()
    save.wait()


def on_device(inputs, grad_out, gate_pre, up_pre, w_gate, w_up, w_down):
    anywhere = pl.BlockSpec(memory_space=pl.ANY)
    vmem = pl.BlockSpec(memory_space=pltpu.VMEM)
    tokens = pltpu.VMEM((2 * R, RB, DS), BF16)
    nsem = 14 + 60 + 48 * len(CHUNKS) + 4
    hidden, grads, inp_all, go_all, gi = pl.pallas_call(
        comm_kernel,
        out_shape=(
            pltpu.VMEM((R, R, TB, FFS), BF16), pltpu.VMEM((2, R, R, TB, FFS), BF16), tokens, tokens,
            pltpu.VMEM((RB, DS), BF16),
        ),
        in_specs=[anywhere] * 7,
        out_specs=[vmem] * 5,
        scratch_shapes=[
            pltpu.VMEM((TB, FFS), BF16),
            pltpu.VMEM((TB, FFS), BF16),
            pltpu.VMEM((DS, FFS), BF16),
            pltpu.VMEM((DS, FFS), BF16),
            pltpu.VMEM((FFS, DS), BF16),
            pltpu.VMEM((R, R, TB, FFS), F32),
            pltpu.VMEM((R, R, TB, FFS), BF16),
            pltpu.VMEM((2, 6, R, QR, HALF), BF16),
            pltpu.VMEM((2, 2, R, QR, HALF), BF16),
            pltpu.VMEM((2, R, TB, HALF), F32),
            pltpu.VMEM((2, R, TB, HALF), BF16),
            pltpu.VMEM((2, 6, QR, HALF), BF16),
            pltpu.VMEM((2, 2, QR, HALF), BF16),
            pltpu.VMEM((R, R, TB, DS), F32),
            pltpu.VMEM((R, 2, TB, DS), F32),
            pltpu.VMEM((3, RB, DS), BF16),
            pltpu.VMEM((3, RB, DS), BF16),
            pltpu.SemaphoreType.DMA((7,)),
            pltpu.SemaphoreType.DMA((nsem,)),
            pltpu.SemaphoreType.DMA((nsem,)),
        ],
        compiler_params=pltpu.CompilerParams(
            collective_id=0, has_side_effects=True, vmem_limit_bytes=46 * 1024 * 1024
        ),
    )(inputs, grad_out, gate_pre, up_pre, w_gate, w_up, w_down)

    return pl.pallas_call(
        weights_kernel,
        out_shape=(
            jax.ShapeDtypeStruct((RB, DS), BF16),
            jax.ShapeDtypeStruct((DS, FFS), BF16),
            jax.ShapeDtypeStruct((DS, FFS), BF16),
            jax.ShapeDtypeStruct((FFS, DS), BF16),
        ),
        in_specs=[vmem] * 5,
        out_specs=[anywhere] * 4,
        scratch_shapes=[
            pltpu.VMEM((2, DS, WT), BF16),
            pltpu.VMEM((2, DS, WT), BF16),
            pltpu.VMEM((2, WT, DS), BF16),
            pltpu.SemaphoreType.DMA((3, 2)),
            pltpu.SemaphoreType.DMA,
        ],
        cost_estimate=pl.CostEstimate(flops=6 * 512 * DS * FFS, bytes_accessed=12 * DS * FFS, transcendentals=0),
        compiler_params=pltpu.CompilerParams(vmem_limit_bytes=32 * 1024 * 1024),
    )(inp_all, go_all, hidden, grads, gi)


def solution(mesh):
    placed = (
        P("row", "col"),
        P("row", "col"),
        P("col", "row"),
        P("col", "row"),
        P("col", "row"),
        P("col", "row"),
        P("row", "col"),
    )
    return jax.shard_map(
        on_device,
        mesh=mesh,
        in_specs=placed,
        out_specs=(P("row", "col"), P("col", "row"), P("col", "row"), P("row", "col")),
        check_vma=False,
    )
```

```python
import jax
import jax.numpy as jnp
from jax import lax
from jax.experimental import pallas as pl
from jax.experimental.pallas import tpu as pltpu
from jax.sharding import PartitionSpec as P

MESH = pl.DeviceIdType.MESH
F32, BF16 = jnp.float32, jnp.bfloat16
NT = (((1,), (1,)), ((), ()))
TN = (((0,), (0,)), ((), ()))
R = 4
TB = 32
FFS = 3584
HALF = FFS // 2
QR = TB // 2
DS = 512
RB = 64


CHUNKS = (4, 4, 4, 2)
FAR = 2
LAG = 1


def comm_kernel(
    inp_ref, go_ref, gp_ref, up_ref, wg_ref, wu_ref, wd_ref,
    dg, du, dd, gi,
    hid_all, g_all, inp_all, inp_t, go_all, gp, up, wg, wu, wd,
    p32, p16, r1, s1, m32, m16, r2, s2, acc, sib, zout, zin,
    loc, ss, rs,
):
    col, row = lax.axis_index("col"), lax.axis_index("row")
    y, x = col // R, lax.rem(col, R)
    z, core = row // 2, lax.rem(row, 2)
    sems = [0]

    def take(n):
        sems[0] += n
        return sems[0] - n

    def add(p, k):
        return lax.rem(p + k, R)

    def at(axis, k):
        return {"col": y * R + add(x, k)} if axis == "x" else {"col": add(y, k) * R + x}

    zdev = [{"row": add(z, k) * 2 + core} for k in (1, 2, 3)]
    other = {"row": z * 2 + 1 - core}

    def rc(k, src, dst, dev):
        return pltpu.make_async_remote_copy(
            src_ref=src, dst_ref=dst, send_sem=ss.at[k], recv_sem=rs.at[k], device_id=dev, device_id_type=MESH
        )

    def got(k, ref):
        rc(k, ref, ref, other).wait_recv()

    def sent(k, ref):
        rc(k, ref, ref, other).wait_send()

    def lc(k, src, dst):
        return pltpu.make_async_copy(src, dst, loc.at[k])

    loads = [
        lc(0, go_ref, go_all.at[row]), lc(1, gp_ref, gp), lc(2, up_ref, up), lc(3, wd_ref, wd),
        lc(4, inp_ref, inp_all.at[row]), lc(5, wg_ref, wg), lc(6, wu_ref, wu),
    ]
    for c in loads:
        c.start()

    barrier = pltpu.get_barrier_semaphore()
    peers = [at("x", 1), at("x", 3), at("y", 1), at("y", 3), other] + zdev
    for d in peers:
        pl.semaphore_signal(barrier, inc=1, device_id=d, device_id_type=MESH)
    pl.semaphore_wait(barrier, len(peers))

    class RowGather:
        def __init__(self, ref):
            self.b, self.ref = take(7), ref

        def start(self):
            for i in range(3):
                rc(self.b + i, self.ref.at[row], self.ref.at[row], zdev[i]).start()
            rc(self.b + 3, self.ref.at[row], self.ref.at[row], other).start()

        def src(self, i):
            return self.ref.at[add(z, 3 - i) * 2 + core]

        def forward(self):
            for i in range(3):
                got(self.b + i, self.src(i))
                rc(self.b + 4 + i, self.src(i), self.src(i), other).start()

        def finish(self):
            for i in range(3, 7):
                got(self.b + i, self.ref.at[row])
            for i in range(7):
                sent(self.b + i, self.ref.at[row])

    class Gather:
        def __init__(self, axis, view):
            self.b, self.axis, self.view = take(6), axis, view
            self.me = x if axis == "x" else y

        def start(self):
            b, v, me = self.b, self.view, self.me
            for k, q, step in ((0, 0, 1), (1, 1, 3), (2, 1, 1), (3, 0, 3)):
                rc(b + k, v(me, q), v(me, q), at(self.axis, step)).start()

        def forward(self):
            b, v, me = self.b, self.view, self.me
            got(b, v(add(me, 3), 0))
            rc(b + 4, v(add(me, 3), 0), v(add(me, 3), 0), at(self.axis, 1)).start()
            got(b + 1, v(add(me, 1), 1))
            rc(b + 5, v(add(me, 1), 1), v(add(me, 1), 1), at(self.axis, 3)).start()

        def near(self):
            got(self.b + 2, self.view(add(self.me, 3), 1))
            got(self.b + 3, self.view(add(self.me, 1), 0))

        def far(self):
            got(self.b + 4, self.view(add(self.me, 2), 0))
            got(self.b + 5, self.view(add(self.me, 2), 1))

        def drain(self):
            for k in range(6):
                sent(self.b + k, self.view(self.me, 0))

    class Scatter:
        def __init__(self, axis, wide, narrow, recv, send):
            self.b, self.axis, self.wide, self.narrow, self.recv, self.send = take(6), axis, wide, narrow, recv, send
            self.me = x if axis == "x" else y

        def start(self):
            me = self.me
            for k, d, q, step in ((0, 2, 0, 1), (1, 2, 1, 3), (2, 1, 1, 1), (3, 3, 0, 3)):
                rc(self.b + k, self.narrow(add(me, d), q), self.recv(k), at(self.axis, step)).start()

        def forward(self):
            me = self.me
            for k, d, q, step in ((0, 1, 0, 1), (1, 3, 1, 3)):
                got(self.b + k, self.recv(k))
                part = self.wide(add(me, d), q)[...] + self.recv(k)[...].astype(F32)
                self.send(k)[...] = part.astype(self.send(k).dtype)
                rc(self.b + 4 + k, self.send(k), self.recv(4 + k), at(self.axis, step)).start()

        def result(self, q):
            i, k = (3, 4) if q == 0 else (2, 5)
            got(self.b + i, self.recv(i))
            got(self.b + k, self.recv(k))
            return self.wide(self.me, q)[...] + self.recv(i)[...].astype(F32) + self.recv(k)[...].astype(F32)

        def drain(self):
            for k in range(6):
                sent(self.b + k, self.recv(0))

    def gathers(c, h, one):
        if h == 0:
            return Gather("x", lambda p, q: one(y, p, q, c)), Gather("y", lambda p, q: one(p, slice(None), q, c))
        return Gather("y", lambda p, q: one(p, x, q, c)), Gather("x", lambda p, q: one(slice(None), p, q, c))

    def rows(q):
        return pl.ds(q * QR, QR)

    class Chunk:
        def __init__(self, j):
            self.w = CHUNKS[j] * 128
            self.o, self.ho = 256 * sum(CHUNKS[:j]), 128 * sum(CHUNKS[:j])
            self.red1, self.red2, self.gat = [], [], []
            hc = pl.ds(self.ho, self.w)
            for h in range(2):
                c = self.cols(h)
                pick = (lambda ref, d, q, c=c: ref.at[d, :, rows(q), c]) if h == 0 else (
                    lambda ref, d, q, c=c: ref.at[:, d, rows(q), c])
                self.red1.append(Scatter(
                    "yx"[h], lambda d, q, f=pick: f(p32, d, q), lambda d, q, f=pick: f(p16, d, q),
                    lambda k, h=h: r1.at[h, k, :, :, hc], lambda k, h=h: s1.at[h, k, :, :, hc]))
                self.red2.append(Scatter(
                    "xy"[h], lambda d, q, h=h: m32.at[h, d, rows(q), hc], lambda d, q, h=h: m16.at[h, d, rows(q), hc],
                    lambda k, h=h: r2.at[h, k, :, hc], lambda k, h=h: s2.at[h, k, :, hc]))
                self.gat.append(gathers(c, h, lambda a, b, q, c: g_all.at[:, a, b, rows(q), c]))
            self.hc = hc

        def cols(self, h):
            return pl.ds(self.o + h * self.w, self.w)

        def product(self):
            def body(i, t):
                c = pl.ds(pl.multiple_of(self.o + i * 256, 256), 256)
                v = lax.dot_general(
                    go_all[...].reshape(512, DS), wd[c, :], NT, preferred_element_type=F32
                ).reshape(R, R, TB, 256)
                p32[:, :, :, c] = v
                p16[:, :, :, c] = v.astype(BF16)
                return t

            lax.fori_loop(0, self.w // 128, body, 0)

        def step(self, s):
            for h in range(2):
                if s == 0:
                    if h == 0:
                        self.product()
                    self.red1[h].start()
                if s == 1:
                    self.red1[h].forward()
                if s == 2:
                    for q in range(2):
                        v = self.red1[h].result(q)
                        m32[h, :, rows(q), self.hc] = v
                        m16[h, :, rows(q), self.hc] = v.astype(BF16)
                    self.red2[h].start()
                if s == 3:
                    self.red2[h].forward()
                if s == 4:
                    c = self.cols(h)
                    for q in range(2):
                        hg = self.red2[h].result(q)
                        gw, uw = gp[rows(q), c].astype(F32), up[rows(q), c].astype(F32)
                        sg = jax.nn.sigmoid(gw)
                        g_all[0, y, x, rows(q), c] = (hg * uw * sg * (1.0 + gw * (1.0 - sg))).astype(BF16)
                        g_all[1, y, x, rows(q), c] = (hg * (gw * sg)).astype(BF16)
                    self.gat[h][0].start()
                if s == 5:
                    self.gat[h][0].forward()
                if s == 6:
                    self.gat[h][0].near()
                    self.gat[h][0].far()
                    self.gat[h][1].start()
                if s == 7:
                    self.gat[h][1].forward()
                if s == 8:
                    self.gat[h][1].near()
                    self.gat[h][1].far()
            if s == 9:
                c = pl.ds(self.o, 2 * self.w)
                for a, w in ((0, wg), (1, wu)):
                    lhs = g_all[a, :, :, :, c].reshape(512, 2 * self.w)
                    acc[...] += lax.dot_general(
                        lhs, w[:, c], NT, preferred_element_type=F32).reshape(R, R, TB, DS)

        def weights(self):
            def body(i, t):
                c = pl.ds(pl.multiple_of(self.o + i * 256, 256), 256)
                for a, d in ((0, dg), (1, du)):
                    v = g_all[a, :, :, :, c].reshape(512, 256)
                    d[:, c] = jnp.dot(inp_t[...], v, preferred_element_type=F32).astype(BF16)
                return t

            lax.fori_loop(0, self.w // 128, body, 0)

        def drain(self):
            for h in range(2):
                for t in (self.red1[h], self.red2[h], *self.gat[h]):
                    t.drain()

    go_gather, inp_gather = RowGather(go_all), RowGather(inp_all)
    hid = []
    for h in range(2):
        view = lambda a, b, q, h=h: hid_all.at[a, b, rows(q), pl.ds(h * HALF, HALF)]
        if h == 0:
            hid.append((Gather("x", lambda p, q, v=view: v(y, p, q)), [
                Gather("y", lambda p, q, v=view, k=k: v(p, add(x, k), q)) for k in range(R)]))
        else:
            hid.append((Gather("y", lambda p, q, v=view: v(p, x, q)), [
                Gather("x", lambda p, q, v=view, k=k: v(add(y, k), p, q)) for k in range(R)]))
    chunks = [Chunk(j) for j in range(len(CHUNKS))]
    rowsum = take(4)

    loads[0].wait()
    go_gather.start()
    loads[4].wait()
    inp_gather.start()

    loads[1].wait()
    loads[2].wait()
    gw, uw = gp[...].astype(F32), up[...].astype(F32)
    hid_all[y, x] = (gw * jax.nn.sigmoid(gw) * uw).astype(BF16)
    for f, s in hid:
        f.start()
        s[0].start()
    acc[...] = jnp.zeros_like(acc)
    for f, s in hid:
        f.forward()
        f.near()
        s[1].start()
        s[3].start()
    go_gather.forward()
    go_gather.finish()
    for c in loads[3:4] + loads[5:]:
        c.wait()

    last = 8 + LAG * (len(CHUNKS) - 1)
    for t in range(last + 1):
        for j, chunk in enumerate(chunks):
            if 0 <= t - LAG * j <= 8:
                chunk.step(t - LAG * j)
        if t == 0:
            inp_gather.forward()
        if t == 4:
            inp_gather.finish()
            inp_t[...] = inp_all[...].reshape(512, DS).T
        for f, s in hid:
            if t == last - FAR:
                f.far()
                s[2].start()
            if t == last - 1:
                for k in (0, 1, 3):
                    s[k].forward()
            if t == last:
                s[2].forward()
        for j, chunk in enumerate(chunks):
            if t - LAG * j == 8:
                chunk.step(9)
                if t < last:
                    chunk.weights()

    rc(rowsum, acc.at[:, pl.ds(2 * (1 - core), 2)], sib, other).start()
    chunks[-1].weights()
    got(rowsum, sib)
    for i in range(3):
        p = add(z, i + 1)
        zout[i] = (acc[p, pl.ds(2 * core, 2)] + sib[p]).reshape(RB, DS).astype(BF16)
        rc(rowsum + 1 + i, zout.at[i], zin.at[i], zdev[i]).start()
    total = (acc[z, pl.ds(2 * core, 2)] + sib[z]).reshape(RB, DS)
    for f, s in hid:
        for g in s:
            g.near()
            g.far()

    def down(i, t):
        c = pl.ds(pl.multiple_of(i * 512, 512), 512)
        v = hid_all[:, :, :, c].reshape(512, 512)
        dd[c, :] = lax.dot_general(v, go_all[...].reshape(512, DS), TN, preferred_element_type=F32).astype(BF16)
        return t

    lax.fori_loop(0, FFS // 512, down, 0)
    for f, s in hid:
        for g in [f] + s:
            g.drain()
    for chunk in chunks:
        chunk.drain()
    for i in range(3):
        got(rowsum + 1 + i, zin.at[i])
        total = total + zin[i].astype(F32)
    gi[...] = total.astype(BF16)
    sent(rowsum, sib)
    for i in range(3):
        sent(rowsum + 1 + i, zout.at[i])


def store_kernel(dg, du, dd, gi, dg_ref, du_ref, dd_ref, gi_ref, sem):
    pairs = ((dg, dg_ref), (du, du_ref), (dd, dd_ref), (gi, gi_ref))
    copies = [pltpu.make_async_copy(a, b, sem.at[i]) for i, (a, b) in enumerate(pairs)]
    for c in copies:
        c.start()
    for c in copies:
        c.wait()


def on_device(inputs, grad_out, gate_pre, up_pre, w_gate, w_up, w_down):
    anywhere = pl.BlockSpec(memory_space=pl.ANY)
    vmem = pl.BlockSpec(memory_space=pltpu.VMEM)
    shapes = ((DS, FFS), (DS, FFS), (FFS, DS), (RB, DS))
    nsem = 14 + 60 + 48 * len(CHUNKS) + 4
    dg, du, dd, gi = pl.pallas_call(
        comm_kernel,
        out_shape=[pltpu.VMEM(v, BF16) for v in shapes],
        in_specs=[anywhere] * 7,
        out_specs=[vmem] * 4,
        scratch_shapes=[
            pltpu.VMEM((R, R, TB, FFS), BF16),
            pltpu.VMEM((2, R, R, TB, FFS), BF16),
            pltpu.VMEM((2 * R, RB, DS), BF16),
            pltpu.VMEM((DS, 512), BF16),
            pltpu.VMEM((2 * R, RB, DS), BF16),
            pltpu.VMEM((TB, FFS), BF16),
            pltpu.VMEM((TB, FFS), BF16),
            pltpu.VMEM((DS, FFS), BF16),
            pltpu.VMEM((DS, FFS), BF16),
            pltpu.VMEM((FFS, DS), BF16),
            pltpu.VMEM((R, R, TB, FFS), F32),
            pltpu.VMEM((R, R, TB, FFS), BF16),
            pltpu.VMEM((2, 6, R, QR, HALF), BF16),
            pltpu.VMEM((2, 2, R, QR, HALF), BF16),
            pltpu.VMEM((2, R, TB, HALF), F32),
            pltpu.VMEM((2, R, TB, HALF), BF16),
            pltpu.VMEM((2, 6, QR, HALF), BF16),
            pltpu.VMEM((2, 2, QR, HALF), BF16),
            pltpu.VMEM((R, R, TB, DS), F32),
            pltpu.VMEM((R, 2, TB, DS), F32),
            pltpu.VMEM((3, RB, DS), BF16),
            pltpu.VMEM((3, RB, DS), BF16),
            pltpu.SemaphoreType.DMA((7,)),
            pltpu.SemaphoreType.DMA((nsem,)),
            pltpu.SemaphoreType.DMA((nsem,)),
        ],
        compiler_params=pltpu.CompilerParams(
            collective_id=0, has_side_effects=True, vmem_limit_bytes=50 * 1024 * 1024
        ),
    )(inputs, grad_out, gate_pre, up_pre, w_gate, w_up, w_down)

    dg, du, dd, gi = pl.pallas_call(
        store_kernel,
        out_shape=[jax.ShapeDtypeStruct(v, BF16) for v in shapes],
        in_specs=[vmem] * 4,
        out_specs=[anywhere] * 4,
        scratch_shapes=[pltpu.SemaphoreType.DMA((4,))],
        compiler_params=pltpu.CompilerParams(vmem_limit_bytes=4 * 1024 * 1024),
    )(dg, du, dd, gi)
    return (gi, dg, du, dd)


def solution(mesh):
    placed = (
        P("row", "col"),
        P("row", "col"),
        P("col", "row"),
        P("col", "row"),
        P("col", "row"),
        P("col", "row"),
        P("row", "col"),
    )
    return jax.shard_map(
        on_device,
        mesh=mesh,
        in_specs=placed,
        out_specs=(P("row", "col"), P("col", "row"), P("col", "row"), P("row", "col")),
        check_vma=False,
    )
```

```python
import jax
import jax.numpy as jnp
from jax import lax
from jax.experimental import pallas as pl
from jax.experimental.pallas import tpu as pltpu
from jax.sharding import PartitionSpec as P

MESH = pl.DeviceIdType.MESH
F32, BF16 = jnp.float32, jnp.bfloat16
NT = (((1,), (1,)), ((), ()))
TN = (((0,), (0,)), ((), ()))
R = 4
TB = 32
FFS = 3584
HALF = FFS // 2
QR = TB // 2
DS = 512
RB = 64


CHUNKS = (4, 4, 4, 2)
LAG_SUM = 0.6
LAG_GATHER = 0.6
NEAR = -1
FAR = 0.4
AHEAD = 1.0


def comm_kernel(
    inp_ref, go_ref, gp_ref, up_ref, wg_ref, wu_ref, wd_ref,
    dg, du, dd, gi,
    hid_all, g_all, inp_all, inp_t, go_all, gp, up, wg, wu, wd,
    p32, p16, r1, s1, m32, m16, r2, s2, acc, sib, zout, zin,
    loc, ss, rs,
):
    col, row = lax.axis_index("col"), lax.axis_index("row")
    y, x = col // R, lax.rem(col, R)
    z, core = row // 2, lax.rem(row, 2)
    sems = [0]

    def take(n):
        sems[0] += n
        return sems[0] - n

    def add(p, k):
        return lax.rem(p + k, R)

    def at(axis, k):
        return {"col": y * R + add(x, k)} if axis == "x" else {"col": add(y, k) * R + x}

    zdev = [{"row": add(z, k) * 2 + core} for k in (1, 2, 3)]
    other = {"row": z * 2 + 1 - core}
    zfar = [[{"row": add(z, k) * 2 + lax.rem(core + j, 2)} for j in range(2)] for k in (1, 2, 3)]

    def rc(k, src, dst, dev):
        return pltpu.make_async_remote_copy(
            src_ref=src, dst_ref=dst, send_sem=ss.at[k], recv_sem=rs.at[k], device_id=dev, device_id_type=MESH
        )

    def got(k, ref):
        rc(k, ref, ref, other).wait_recv()

    def sent(k, ref):
        rc(k, ref, ref, other).wait_send()

    def lc(k, src, dst):
        return pltpu.make_async_copy(src, dst, loc.at[k])

    loads = [
        lc(0, go_ref, go_all.at[row]), lc(1, gp_ref, gp), lc(2, up_ref, up), lc(3, wd_ref, wd),
        lc(4, inp_ref, inp_all.at[row]), lc(5, wg_ref, wg), lc(6, wu_ref, wu),
    ]
    for c in loads:
        c.start()

    barrier = pltpu.get_barrier_semaphore()
    peers = [at("x", 1), at("x", 3), at("y", 1), at("y", 3), other] + sum(zfar, [])
    for d in peers:
        pl.semaphore_signal(barrier, inc=1, device_id=d, device_id_type=MESH)
    pl.semaphore_wait(barrier, len(peers))

    class RowGather:
        def __init__(self, ref):
            self.b, self.ref = take(7), ref

        def start(self):
            for i in range(3):
                rc(self.b + i, self.ref.at[row], self.ref.at[row], zdev[i]).start()
            rc(self.b + 3, self.ref.at[row], self.ref.at[row], other).start()

        def src(self, i):
            return self.ref.at[add(z, 3 - i) * 2 + core]

        def forward(self):
            for i in range(3):
                got(self.b + i, self.src(i))
                rc(self.b + 4 + i, self.src(i), self.src(i), other).start()

        def finish(self):
            for i in range(3, 7):
                got(self.b + i, self.ref.at[row])
            for i in range(7):
                sent(self.b + i, self.ref.at[row])

    class Gather:
        def __init__(self, axis, view):
            self.b, self.axis, self.view = take(6), axis, view
            self.me = x if axis == "x" else y

        def start(self):
            b, v, me = self.b, self.view, self.me
            for k, q, step in ((0, 0, 1), (1, 1, 3), (2, 1, 1), (3, 0, 3)):
                rc(b + k, v(me, q), v(me, q), at(self.axis, step)).start()

        def forward(self):
            b, v, me = self.b, self.view, self.me
            got(b, v(add(me, 3), 0))
            rc(b + 4, v(add(me, 3), 0), v(add(me, 3), 0), at(self.axis, 1)).start()
            got(b + 1, v(add(me, 1), 1))
            rc(b + 5, v(add(me, 1), 1), v(add(me, 1), 1), at(self.axis, 3)).start()

        def near(self):
            got(self.b + 2, self.view(add(self.me, 3), 1))
            got(self.b + 3, self.view(add(self.me, 1), 0))

        def far(self):
            got(self.b + 4, self.view(add(self.me, 2), 0))
            got(self.b + 5, self.view(add(self.me, 2), 1))

        def drain(self):
            for k in range(6):
                sent(self.b + k, self.view(self.me, 0))

    class Scatter:
        def __init__(self, axis, wide, narrow, recv, send):
            self.b, self.axis, self.wide, self.narrow, self.recv, self.send = take(6), axis, wide, narrow, recv, send
            self.me = x if axis == "x" else y

        def start(self):
            me = self.me
            for k, d, q, step in ((0, 2, 0, 1), (1, 2, 1, 3), (2, 1, 1, 1), (3, 3, 0, 3)):
                rc(self.b + k, self.narrow(add(me, d), q), self.recv(k), at(self.axis, step)).start()

        def forward(self):
            me = self.me
            for k, d, q, step in ((0, 1, 0, 1), (1, 3, 1, 3)):
                got(self.b + k, self.recv(k))
                part = self.wide(add(me, d), q)[...] + self.recv(k)[...].astype(F32)
                self.send(k)[...] = part.astype(self.send(k).dtype)
                rc(self.b + 4 + k, self.send(k), self.recv(4 + k), at(self.axis, step)).start()

        def result(self, q):
            i, k = (3, 4) if q == 0 else (2, 5)
            got(self.b + i, self.recv(i))
            got(self.b + k, self.recv(k))
            return self.wide(self.me, q)[...] + self.recv(i)[...].astype(F32) + self.recv(k)[...].astype(F32)

        def drain(self):
            for k in range(6):
                sent(self.b + k, self.recv(0))

    def gathers(c, h, one):
        if h == 0:
            return Gather("x", lambda p, q: one(y, p, q, c)), Gather("y", lambda p, q: one(p, slice(None), q, c))
        return Gather("y", lambda p, q: one(p, x, q, c)), Gather("x", lambda p, q: one(slice(None), p, q, c))

    def rows(q):
        return pl.ds(q * QR, QR)

    class Chunk:
        def __init__(self, j):
            self.w = CHUNKS[j] * 128
            self.o, self.ho = 256 * sum(CHUNKS[:j]), 128 * sum(CHUNKS[:j])
            self.red1, self.red2, self.gat = [], [], []
            hc = pl.ds(self.ho, self.w)
            for h in range(2):
                c = self.cols(h)
                pick = (lambda ref, d, q, c=c: ref.at[d, :, rows(q), c]) if h == 0 else (
                    lambda ref, d, q, c=c: ref.at[:, d, rows(q), c])
                self.red1.append(Scatter(
                    "yx"[h], lambda d, q, f=pick: f(p32, d, q), lambda d, q, f=pick: f(p16, d, q),
                    lambda k, h=h: r1.at[h, k, :, :, hc], lambda k, h=h: s1.at[h, k, :, :, hc]))
                self.red2.append(Scatter(
                    "xy"[h], lambda d, q, h=h: m32.at[h, d, rows(q), hc], lambda d, q, h=h: m16.at[h, d, rows(q), hc],
                    lambda k, h=h: r2.at[h, k, :, hc], lambda k, h=h: s2.at[h, k, :, hc]))
                self.gat.append(gathers(c, h, lambda a, b, q, c: g_all.at[:, a, b, rows(q), c]))
            self.hc = hc

        def cols(self, h):
            return pl.ds(self.o + h * self.w, self.w)

        def product(self):
            def body(i, t):
                c = pl.ds(pl.multiple_of(self.o + i * 256, 256), 256)
                v = lax.dot_general(
                    go_all[...].reshape(512, DS), wd[c, :], NT, preferred_element_type=F32
                ).reshape(R, R, TB, 256)
                p32[:, :, :, c] = v
                p16[:, :, :, c] = v.astype(BF16)
                return t

            lax.fori_loop(0, self.w // 128, body, 0)

        def step(self, s):
            for h in range(2):
                if s == 0:
                    if h == 0:
                        self.product()
                    self.red1[h].start()
                if s == 1:
                    self.red1[h].forward()
                if s == 2:
                    for q in range(2):
                        v = self.red1[h].result(q)
                        m32[h, :, rows(q), self.hc] = v
                        m16[h, :, rows(q), self.hc] = v.astype(BF16)
                    self.red2[h].start()
                if s == 3:
                    self.red2[h].forward()
                if s == 4:
                    c = self.cols(h)
                    for q in range(2):
                        hg = self.red2[h].result(q)
                        gw, uw = gp[rows(q), c].astype(F32), up[rows(q), c].astype(F32)
                        sg = jax.nn.sigmoid(gw)
                        g_all[0, y, x, rows(q), c] = (hg * uw * sg * (1.0 + gw * (1.0 - sg))).astype(BF16)
                        g_all[1, y, x, rows(q), c] = (hg * (gw * sg)).astype(BF16)
                    self.gat[h][0].start()
                if s == 5:
                    self.gat[h][0].forward()
                if s == 6:
                    self.gat[h][0].near()
                    self.gat[h][0].far()
                    self.gat[h][1].start()
                if s == 7:
                    self.gat[h][1].forward()
                if s == 8:
                    self.gat[h][1].near()
                    self.gat[h][1].far()
            if s == 9:
                c = pl.ds(self.o, 2 * self.w)
                for a, w in ((0, wg), (1, wu)):
                    lhs = g_all[a, :, :, :, c].reshape(512, 2 * self.w)
                    acc[...] += lax.dot_general(
                        lhs, w[:, c], NT, preferred_element_type=F32).reshape(R, R, TB, DS)

        def weights(self):
            def body(i, t):
                c = pl.ds(pl.multiple_of(self.o + i * 256, 256), 256)
                for a, d in ((0, dg), (1, du)):
                    v = g_all[a, :, :, :, c].reshape(512, 256)
                    d[:, c] = jnp.dot(inp_t[...], v, preferred_element_type=F32).astype(BF16)
                return t

            lax.fori_loop(0, self.w // 128, body, 0)

        def drain(self):
            for h in range(2):
                for t in (self.red1[h], self.red2[h], *self.gat[h]):
                    t.drain()

    go_gather, inp_gather = RowGather(go_all), RowGather(inp_all)
    hid = []
    for h in range(2):
        view = lambda a, b, q, h=h: hid_all.at[a, b, rows(q), pl.ds(h * HALF, HALF)]
        if h == 0:
            hid.append((Gather("x", lambda p, q, v=view: v(y, p, q)), [
                Gather("y", lambda p, q, v=view, k=k: v(p, add(x, k), q)) for k in range(R)]))
        else:
            hid.append((Gather("y", lambda p, q, v=view: v(p, x, q)), [
                Gather("x", lambda p, q, v=view, k=k: v(add(y, k), p, q)) for k in range(R)]))
    chunks = [Chunk(j) for j in range(len(CHUNKS))]
    rowsum = take(7)

    loads[0].wait()
    go_gather.start()
    loads[4].wait()
    inp_gather.start()

    loads[1].wait()
    loads[2].wait()
    gw, uw = gp[...].astype(F32), up[...].astype(F32)
    hid_all[y, x] = (gw * jax.nn.sigmoid(gw) * uw).astype(BF16)
    for f, s in hid:
        f.start()
        s[0].start()
    acc[...] = jnp.zeros_like(acc)
    for f, s in hid:
        f.forward()
        f.near()
        s[1].start()
    go_gather.forward()
    go_gather.finish()
    for c in loads[3:4] + loads[5:]:
        c.wait()

    def place(j, s):
        return s + (LAG_SUM if s < 4 else LAG_GATHER) * j

    def hid_near():
        for f, s in hid:
            s[3].start()

    def hid_far():
        for f, s in hid:
            f.far()
            s[2].start()

    def hid_ahead():
        for f, s in hid:
            for k in (0, 1, 3):
                s[k].forward()

    def hid_last():
        for f, s in hid:
            s[2].forward()

    def turn():
        inp_gather.finish()
        inp_t[...] = inp_all[...].reshape(512, DS).T

    n = len(CHUNKS)
    end = place(n - 1, 8)
    plan = [(0.5, inp_gather.forward), (3.5, turn), (NEAR, hid_near)]
    plan += [(end - AHEAD + 0.1, hid_ahead), (end - AHEAD - FAR, hid_far), (end + 0.1, hid_last), (end + 0.2, lambda: chunks[-1].step(9))]
    for j, chunk in enumerate(chunks):
        plan += [(place(j, s), lambda c=chunk, s=s: c.step(s)) for s in range(9)]
        if j < n - 1:
            plan += [(place(j, 8) + 0.3, lambda c=chunk: c.step(9)), (place(j, 8) + 0.3, chunk.weights)]
    for _, act in sorted(plan, key=lambda v: v[0]):
        act()

    zout[...] = acc[...].reshape(R, 2, RB, DS).astype(BF16)
    for i in range(3):
        for j in range(2):
            rc(rowsum + 1 + 2 * i + j, zout.at[add(z, i + 1), lax.rem(core + j, 2)], zin.at[i, j], zfar[i][j]).start()
    rc(rowsum, acc.at[z, pl.ds(2 * (1 - core), 2)], sib, other).start()
    chunks[-1].weights()
    got(rowsum, sib)
    total = (acc[z, pl.ds(2 * core, 2)] + sib[...]).reshape(RB, DS)
    for f, s in hid:
        for g in s:
            g.near()
            g.far()

    def down(i, t):
        c = pl.ds(pl.multiple_of(i * 512, 512), 512)
        v = hid_all[:, :, :, c].reshape(512, 512)
        dd[c, :] = lax.dot_general(v, go_all[...].reshape(512, DS), TN, preferred_element_type=F32).astype(BF16)
        return t

    lax.fori_loop(0, FFS // 512, down, 0)
    for f, s in hid:
        for g in [f] + s:
            g.drain()
    for chunk in chunks:
        chunk.drain()
    for i in range(3):
        for j in range(2):
            got(rowsum + 1 + 2 * i + j, zin.at[i, j])
            total = total + zin[i, j].astype(F32)
    gi[...] = total.astype(BF16)
    sent(rowsum, sib)
    for i in range(6):
        sent(rowsum + 1 + i, zin.at[0, 0])


def store_kernel(dg, du, dd, gi, dg_ref, du_ref, dd_ref, gi_ref, sem):
    pairs = ((dg, dg_ref), (du, du_ref), (dd, dd_ref), (gi, gi_ref))
    copies = [pltpu.make_async_copy(a, b, sem.at[i]) for i, (a, b) in enumerate(pairs)]
    for c in copies:
        c.start()
    for c in copies:
        c.wait()


def on_device(inputs, grad_out, gate_pre, up_pre, w_gate, w_up, w_down):
    anywhere = pl.BlockSpec(memory_space=pl.ANY)
    vmem = pl.BlockSpec(memory_space=pltpu.VMEM)
    shapes = ((DS, FFS), (DS, FFS), (FFS, DS), (RB, DS))
    nsem = 14 + 60 + 48 * len(CHUNKS) + 7
    dg, du, dd, gi = pl.pallas_call(
        comm_kernel,
        out_shape=[pltpu.VMEM(v, BF16) for v in shapes],
        in_specs=[anywhere] * 7,
        out_specs=[vmem] * 4,
        scratch_shapes=[
            pltpu.VMEM((R, R, TB, FFS), BF16),
            pltpu.VMEM((2, R, R, TB, FFS), BF16),
            pltpu.VMEM((2 * R, RB, DS), BF16),
            pltpu.VMEM((DS, 512), BF16),
            pltpu.VMEM((2 * R, RB, DS), BF16),
            pltpu.VMEM((TB, FFS), BF16),
            pltpu.VMEM((TB, FFS), BF16),
            pltpu.VMEM((DS, FFS), BF16),
            pltpu.VMEM((DS, FFS), BF16),
            pltpu.VMEM((FFS, DS), BF16),
            pltpu.VMEM((R, R, TB, FFS), F32),
            pltpu.VMEM((R, R, TB, FFS), BF16),
            pltpu.VMEM((2, 6, R, QR, HALF), BF16),
            pltpu.VMEM((2, 2, R, QR, HALF), BF16),
            pltpu.VMEM((2, R, TB, HALF), F32),
            pltpu.VMEM((2, R, TB, HALF), BF16),
            pltpu.VMEM((2, 6, QR, HALF), BF16),
            pltpu.VMEM((2, 2, QR, HALF), BF16),
            pltpu.VMEM((R, R, TB, DS), F32),
            pltpu.VMEM((2, TB, DS), F32),
            pltpu.VMEM((R, 2, RB, DS), BF16),
            pltpu.VMEM((3, 2, RB, DS), BF16),
            pltpu.SemaphoreType.DMA((7,)),
            pltpu.SemaphoreType.DMA((nsem,)),
            pltpu.SemaphoreType.DMA((nsem,)),
        ],
        compiler_params=pltpu.CompilerParams(
            collective_id=0, has_side_effects=True, vmem_limit_bytes=50 * 1024 * 1024
        ),
    )(inputs, grad_out, gate_pre, up_pre, w_gate, w_up, w_down)

    dg, du, dd, gi = pl.pallas_call(
        store_kernel,
        out_shape=[jax.ShapeDtypeStruct(v, BF16) for v in shapes],
        in_specs=[vmem] * 4,
        out_specs=[anywhere] * 4,
        scratch_shapes=[pltpu.SemaphoreType.DMA((4,))],
        compiler_params=pltpu.CompilerParams(vmem_limit_bytes=4 * 1024 * 1024),
    )(dg, du, dd, gi)
    return (gi, dg, du, dd)


def solution(mesh):
    placed = (
        P("row", "col"),
        P("row", "col"),
        P("col", "row"),
        P("col", "row"),
        P("col", "row"),
        P("col", "row"),
        P("row", "col"),
    )
    return jax.shard_map(
        on_device,
        mesh=mesh,
        in_specs=placed,
        out_specs=(P("row", "col"), P("col", "row"), P("col", "row"), P("row", "col")),
        check_vma=False,
    )
```

```python
import jax
import jax.numpy as jnp
from jax import lax
from jax.experimental import pallas as pl
from jax.experimental.pallas import tpu as pltpu
from jax.sharding import PartitionSpec as P

MESH = pl.DeviceIdType.MESH
F32, BF16 = jnp.float32, jnp.bfloat16
NT = (((1,), (1,)), ((), ()))
TN = (((0,), (0,)), ((), ()))
R = 4
TB = 32
FFS = 3584
HALF = FFS // 2
QR = TB // 2
DS = 512
RB = 64


CHUNKS = (4, 4, 4, 2)
LAG_SUM = 0.6
LAG_GATHER = 0.6
NEAR = -1
FAR = 0.4
AHEAD = 1.0


def comm_kernel(
    inp_ref, go_ref, gp_ref, up_ref, wg_ref, wu_ref, wd_ref,
    dg, du, dd, gi,
    hid_all, g_all, inp_all, inp_t, go_all, gp, up, wg, wu, wd,
    p32, p16, r1, s1, m32, m16, r2, s2, acc, sib, zout, zin,
    loc, ss, rs,
):
    col, row = lax.axis_index("col"), lax.axis_index("row")
    y, x = col // R, lax.rem(col, R)
    z, core = row // 2, lax.rem(row, 2)
    sems = [0]

    def take(n):
        sems[0] += n
        return sems[0] - n

    def add(p, k):
        return lax.rem(p + k, R)

    def at(axis, k):
        return {"col": y * R + add(x, k)} if axis == "x" else {"col": add(y, k) * R + x}

    zdev = [{"row": add(z, k) * 2 + core} for k in (1, 2, 3)]
    other = {"row": z * 2 + 1 - core}
    zfar = [[{"row": add(z, k) * 2 + lax.rem(core + j, 2)} for j in range(2)] for k in (1, 2, 3)]

    def rc(k, src, dst, dev):
        return pltpu.make_async_remote_copy(
            src_ref=src, dst_ref=dst, send_sem=ss.at[k], recv_sem=rs.at[k], device_id=dev, device_id_type=MESH
        )

    def got(k, ref):
        rc(k, ref, ref, other).wait_recv()

    def sent(k, ref):
        rc(k, ref, ref, other).wait_send()

    def lc(k, src, dst):
        return pltpu.make_async_copy(src, dst, loc.at[k])

    loads = [
        lc(0, go_ref, go_all.at[row]), lc(1, gp_ref, gp), lc(2, up_ref, up), lc(3, wd_ref, wd),
        lc(4, inp_ref, inp_all.at[row]), lc(5, wg_ref, wg), lc(6, wu_ref, wu),
    ]
    for c in loads:
        c.start()

    barrier = pltpu.get_barrier_semaphore()
    peers = [at("x", 1), at("x", 3), at("y", 1), at("y", 3), other] + sum(zfar, [])
    for d in peers:
        pl.semaphore_signal(barrier, inc=1, device_id=d, device_id_type=MESH)
    pl.semaphore_wait(barrier, len(peers))

    class RowGather:
        def __init__(self, ref):
            self.b, self.ref = take(7), ref

        def start(self):
            for i in range(3):
                rc(self.b + i, self.ref.at[row], self.ref.at[row], zdev[i]).start()
            rc(self.b + 3, self.ref.at[row], self.ref.at[row], other).start()

        def src(self, i):
            return self.ref.at[add(z, 3 - i) * 2 + core]

        def forward(self):
            for i in range(3):
                got(self.b + i, self.src(i))
                rc(self.b + 4 + i, self.src(i), self.src(i), other).start()

        def finish(self):
            for i in range(3, 7):
                got(self.b + i, self.ref.at[row])
            for i in range(7):
                sent(self.b + i, self.ref.at[row])

    class Gather:
        def __init__(self, axis, view):
            self.b, self.axis, self.view = take(6), axis, view
            self.me = x if axis == "x" else y

        def start(self):
            b, v, me = self.b, self.view, self.me
            for k, q, step in ((0, 0, 1), (1, 1, 3), (2, 1, 1), (3, 0, 3)):
                rc(b + k, v(me, q), v(me, q), at(self.axis, step)).start()

        def forward(self):
            b, v, me = self.b, self.view, self.me
            got(b, v(add(me, 3), 0))
            rc(b + 4, v(add(me, 3), 0), v(add(me, 3), 0), at(self.axis, 1)).start()
            got(b + 1, v(add(me, 1), 1))
            rc(b + 5, v(add(me, 1), 1), v(add(me, 1), 1), at(self.axis, 3)).start()

        def near(self):
            got(self.b + 2, self.view(add(self.me, 3), 1))
            got(self.b + 3, self.view(add(self.me, 1), 0))

        def far(self):
            got(self.b + 4, self.view(add(self.me, 2), 0))
            got(self.b + 5, self.view(add(self.me, 2), 1))

        def drain(self):
            for k in range(6):
                sent(self.b + k, self.view(self.me, 0))

    class Scatter:
        def __init__(self, axis, wide, narrow, recv, send):
            self.b, self.axis, self.wide, self.narrow, self.recv, self.send = take(6), axis, wide, narrow, recv, send
            self.me = x if axis == "x" else y

        def start(self):
            me = self.me
            for k, d, q, step in ((0, 2, 0, 1), (1, 2, 1, 3), (2, 1, 1, 1), (3, 3, 0, 3)):
                rc(self.b + k, self.narrow(add(me, d), q), self.recv(k), at(self.axis, step)).start()

        def forward(self):
            me = self.me
            for k, d, q, step in ((0, 1, 0, 1), (1, 3, 1, 3)):
                got(self.b + k, self.recv(k))
                part = self.wide(add(me, d), q)[...] + self.recv(k)[...].astype(F32)
                self.send(k)[...] = part.astype(self.send(k).dtype)
                rc(self.b + 4 + k, self.send(k), self.recv(4 + k), at(self.axis, step)).start()

        def result(self, q):
            i, k = (3, 4) if q == 0 else (2, 5)
            got(self.b + i, self.recv(i))
            got(self.b + k, self.recv(k))
            return self.wide(self.me, q)[...] + self.recv(i)[...].astype(F32) + self.recv(k)[...].astype(F32)

        def drain(self):
            for k in range(6):
                sent(self.b + k, self.recv(0))

    def gathers(c, h, one):
        if h == 0:
            return Gather("x", lambda p, q: one(y, p, q, c)), Gather("y", lambda p, q: one(p, slice(None), q, c))
        return Gather("y", lambda p, q: one(p, x, q, c)), Gather("x", lambda p, q: one(slice(None), p, q, c))

    def rows(q):
        return pl.ds(q * QR, QR)

    class Chunk:
        def __init__(self, j):
            self.w = CHUNKS[j] * 128
            self.o, self.ho = 256 * sum(CHUNKS[:j]), 128 * sum(CHUNKS[:j])
            self.red1, self.red2, self.gat = [], [], []
            hc = pl.ds(self.ho, self.w)
            for h in range(2):
                c = self.cols(h)
                pick = (lambda ref, d, q, c=c: ref.at[d, :, rows(q), c]) if h == 0 else (
                    lambda ref, d, q, c=c: ref.at[:, d, rows(q), c])
                self.red1.append(Scatter(
                    "yx"[h], lambda d, q, f=pick: f(p32, d, q), lambda d, q, f=pick: f(p16, d, q),
                    lambda k, h=h: r1.at[h, k, :, :, hc], lambda k, h=h: s1.at[h, k, :, :, hc]))
                self.red2.append(Scatter(
                    "xy"[h], lambda d, q, h=h: m32.at[h, d, rows(q), hc], lambda d, q, h=h: m16.at[h, d, rows(q), hc],
                    lambda k, h=h: r2.at[h, k, :, hc], lambda k, h=h: s2.at[h, k, :, hc]))
                self.gat.append(gathers(c, h, lambda a, b, q, c: g_all.at[:, a, b, rows(q), c]))
            self.hc = hc

        def cols(self, h):
            return pl.ds(self.o + h * self.w, self.w)

        def product(self):
            def body(i, t):
                c = pl.ds(pl.multiple_of(self.o + i * 256, 256), 256)
                v = lax.dot_general(
                    go_all[...].reshape(512, DS), wd[c, :], NT, preferred_element_type=F32
                ).reshape(R, R, TB, 256)
                p32[:, :, :, c] = v
                p16[:, :, :, c] = v.astype(BF16)
                return t

            lax.fori_loop(0, self.w // 128, body, 0)

        def step(self, s):
            for h in range(2):
                if s == 0:
                    if h == 0:
                        self.product()
                    self.red1[h].start()
                if s == 1:
                    self.red1[h].forward()
                if s == 2:
                    for q in range(2):
                        v = self.red1[h].result(q)
                        m32[h, :, rows(q), self.hc] = v
                        m16[h, :, rows(q), self.hc] = v.astype(BF16)
                    self.red2[h].start()
                if s == 3:
                    self.red2[h].forward()
                if s == 4:
                    c = self.cols(h)
                    for q in range(2):
                        hg = self.red2[h].result(q)
                        gw, uw = gp[rows(q), c].astype(F32), up[rows(q), c].astype(F32)
                        sg = jax.nn.sigmoid(gw)
                        g_all[0, y, x, rows(q), c] = (hg * uw * sg * (1.0 + gw * (1.0 - sg))).astype(BF16)
                        g_all[1, y, x, rows(q), c] = (hg * (gw * sg)).astype(BF16)
                    self.gat[h][0].start()
                if s == 5:
                    self.gat[h][0].forward()
                if s == 6:
                    self.gat[h][0].near()
                    self.gat[h][0].far()
                    self.gat[h][1].start()
                if s == 7:
                    self.gat[h][1].forward()
                if s == 8:
                    self.gat[h][1].near()
                    self.gat[h][1].far()
            if s == 9:
                c = pl.ds(self.o, 2 * self.w)
                for a, w in ((0, wg), (1, wu)):
                    lhs = g_all[a, :, :, :, c].reshape(512, 2 * self.w)
                    acc[...] += lax.dot_general(
                        lhs, w[:, c], NT, preferred_element_type=F32).reshape(R, R, TB, DS)

        def weights(self):
            def body(i, t):
                c = pl.ds(pl.multiple_of(self.o + i * 256, 256), 256)
                for a, d in ((0, dg), (1, du)):
                    v = g_all[a, :, :, :, c].reshape(512, 256)
                    d[:, c] = jnp.dot(inp_t[...], v, preferred_element_type=F32).astype(BF16)
                return t

            lax.fori_loop(0, self.w // 128, body, 0)

        def drain(self):
            for h in range(2):
                for t in (self.red1[h], self.red2[h], *self.gat[h]):
                    t.drain()

    go_gather, inp_gather = RowGather(go_all), RowGather(inp_all)
    hid = []
    for h in range(2):
        view = lambda a, b, q, h=h: hid_all.at[a, b, rows(q), pl.ds(h * HALF, HALF)]
        if h == 0:
            hid.append((Gather("x", lambda p, q, v=view: v(y, p, q)), [
                Gather("y", lambda p, q, v=view, k=k: v(p, add(x, k), q)) for k in range(R)]))
        else:
            hid.append((Gather("y", lambda p, q, v=view: v(p, x, q)), [
                Gather("x", lambda p, q, v=view, k=k: v(add(y, k), p, q)) for k in range(R)]))
    chunks = [Chunk(j) for j in range(len(CHUNKS))]
    rowsum = take(7)

    loads[0].wait()
    go_gather.start()

    loads[1].wait()
    loads[2].wait()
    gw, uw = gp[...].astype(F32), up[...].astype(F32)
    hid_all[y, x] = (gw * jax.nn.sigmoid(gw) * uw).astype(BF16)
    for f, s in hid:
        f.start()
        s[0].start()
    acc[...] = jnp.zeros_like(acc)
    for f, s in hid:
        f.forward()
        f.near()
        s[1].start()
    go_gather.forward()
    loads[4].wait()
    inp_gather.start()
    go_gather.finish()
    loads[3].wait()

    def place(j, s):
        return s + (LAG_SUM if s < 4 else LAG_GATHER) * j

    def hid_near():
        for f, s in hid:
            s[3].start()

    def hid_far():
        for f, s in hid:
            f.far()
            s[2].start()

    def hid_ahead():
        for f, s in hid:
            for k in (0, 1, 3):
                s[k].forward()

    def hid_last():
        for f, s in hid:
            s[2].forward()

    def turn():
        loads[5].wait()
        loads[6].wait()
        inp_gather.finish()
        inp_t[...] = inp_all[...].reshape(512, DS).T

    n = len(CHUNKS)
    end = place(n - 1, 8)
    plan = [(1.5, inp_gather.forward), (3.5, turn), (NEAR, hid_near)]
    plan += [(end - AHEAD + 0.1, hid_ahead), (end - AHEAD - FAR, hid_far), (end + 0.1, hid_last), (end + 0.2, lambda: chunks[-1].step(9))]
    for j, chunk in enumerate(chunks):
        plan += [(place(j, s), lambda c=chunk, s=s: c.step(s)) for s in range(9)]
        if j < n - 1:
            plan += [(place(j, 8) + 0.3, lambda c=chunk: c.step(9)), (place(j, 8) + 0.3, chunk.weights)]
    for _, act in sorted(plan, key=lambda v: v[0]):
        act()

    zout[...] = acc[...].reshape(R, 2, RB, DS).astype(BF16)
    for i in range(3):
        for j in range(2):
            rc(rowsum + 1 + 2 * i + j, zout.at[add(z, i + 1), lax.rem(core + j, 2)], zin.at[i, j], zfar[i][j]).start()
    rc(rowsum, acc.at[z, pl.ds(2 * (1 - core), 2)], sib, other).start()
    chunks[-1].weights()
    got(rowsum, sib)
    total = (acc[z, pl.ds(2 * core, 2)] + sib[...]).reshape(RB, DS)
    for f, s in hid:
        for g in s:
            g.near()
            g.far()

    def down(i, t):
        c = pl.ds(pl.multiple_of(i * 512, 512), 512)
        v = hid_all[:, :, :, c].reshape(512, 512)
        dd[c, :] = lax.dot_general(v, go_all[...].reshape(512, DS), TN, preferred_element_type=F32).astype(BF16)
        return t

    lax.fori_loop(0, FFS // 512, down, 0)
    for f, s in hid:
        for g in [f] + s:
            g.drain()
    for chunk in chunks:
        chunk.drain()
    for i in range(3):
        for j in range(2):
            got(rowsum + 1 + 2 * i + j, zin.at[i, j])
            total = total + zin[i, j].astype(F32)
    gi[...] = total.astype(BF16)
    sent(rowsum, sib)
    for i in range(6):
        sent(rowsum + 1 + i, zin.at[0, 0])


def store_kernel(dg, du, dd, gi, dg_ref, du_ref, dd_ref, gi_ref, sem):
    pairs = ((dg, dg_ref), (du, du_ref), (dd, dd_ref), (gi, gi_ref))
    copies = [pltpu.make_async_copy(a, b, sem.at[i]) for i, (a, b) in enumerate(pairs)]
    for c in copies:
        c.start()
    for c in copies:
        c.wait()


def on_device(inputs, grad_out, gate_pre, up_pre, w_gate, w_up, w_down):
    anywhere = pl.BlockSpec(memory_space=pl.ANY)
    vmem = pl.BlockSpec(memory_space=pltpu.VMEM)
    shapes = ((DS, FFS), (DS, FFS), (FFS, DS), (RB, DS))
    nsem = 14 + 60 + 48 * len(CHUNKS) + 7
    dg, du, dd, gi = pl.pallas_call(
        comm_kernel,
        out_shape=[pltpu.VMEM(v, BF16) for v in shapes],
        in_specs=[anywhere] * 7,
        out_specs=[vmem] * 4,
        scratch_shapes=[
            pltpu.VMEM((R, R, TB, FFS), BF16),
            pltpu.VMEM((2, R, R, TB, FFS), BF16),
            pltpu.VMEM((2 * R, RB, DS), BF16),
            pltpu.VMEM((DS, 512), BF16),
            pltpu.VMEM((2 * R, RB, DS), BF16),
            pltpu.VMEM((TB, FFS), BF16),
            pltpu.VMEM((TB, FFS), BF16),
            pltpu.VMEM((DS, FFS), BF16),
            pltpu.VMEM((DS, FFS), BF16),
            pltpu.VMEM((FFS, DS), BF16),
            pltpu.VMEM((R, R, TB, FFS), F32),
            pltpu.VMEM((R, R, TB, FFS), BF16),
            pltpu.VMEM((2, 6, R, QR, HALF), BF16),
            pltpu.VMEM((2, 2, R, QR, HALF), BF16),
            pltpu.VMEM((2, R, TB, HALF), F32),
            pltpu.VMEM((2, R, TB, HALF), BF16),
            pltpu.VMEM((2, 6, QR, HALF), BF16),
            pltpu.VMEM((2, 2, QR, HALF), BF16),
            pltpu.VMEM((R, R, TB, DS), F32),
            pltpu.VMEM((2, TB, DS), F32),
            pltpu.VMEM((R, 2, RB, DS), BF16),
            pltpu.VMEM((3, 2, RB, DS), BF16),
            pltpu.SemaphoreType.DMA((7,)),
            pltpu.SemaphoreType.DMA((nsem,)),
            pltpu.SemaphoreType.DMA((nsem,)),
        ],
        compiler_params=pltpu.CompilerParams(
            collective_id=0, has_side_effects=True, vmem_limit_bytes=50 * 1024 * 1024
        ),
    )(inputs, grad_out, gate_pre, up_pre, w_gate, w_up, w_down)

    dg, du, dd, gi = pl.pallas_call(
        store_kernel,
        out_shape=[jax.ShapeDtypeStruct(v, BF16) for v in shapes],
        in_specs=[vmem] * 4,
        out_specs=[anywhere] * 4,
        scratch_shapes=[pltpu.SemaphoreType.DMA((4,))],
        compiler_params=pltpu.CompilerParams(vmem_limit_bytes=4 * 1024 * 1024),
    )(dg, du, dd, gi)
    return (gi, dg, du, dd)


def solution(mesh):
    placed = (
        P("row", "col"),
        P("row", "col"),
        P("col", "row"),
        P("col", "row"),
        P("col", "row"),
        P("col", "row"),
        P("row", "col"),
    )
    return jax.shard_map(
        on_device,
        mesh=mesh,
        in_specs=placed,
        out_specs=(P("row", "col"), P("col", "row"), P("col", "row"), P("row", "col")),
        check_vma=False,
    )
```
